32 devices in a mesh: groups: 2 (over y), date: 4 (over z), strip: 4 (over x, core).
Axes of the slice: x: 2, y: 2, z: 4, core: 2. Of those that a mesh axis runs over, the one named last changes fastest.
Arguments:
- features: bfloat16 [4, 64, 64, 256], P('date', 'strip', 'groups'), parts along dimension 2, may hold values from -6 to 6
- valid_dates: int32 [4, 64, 64], P('date', 'strip', 'groups'), parts along dimension 2, may hold values from 0 to 1, as said below
- conv_weight: bfloat16 [3, 3, 256, 256], replicated, may hold values from -0.21875 to 0.21875
- conv_bias: float32 [256], replicated, may hold values from -3 to 3
- fade_table: float32 [16], replicated, may hold values from 0.2 to 5
- norm_gain: float32 [256], replicated, may hold values from 0.25 to 4
- w_query: bfloat16 [256, 256], replicated, may hold values from -20 to 20
- w_key: bfloat16 [256, 256], replicated, may hold values from -20 to 20
- w_value: bfloat16 [256, 256], replicated, may hold values from -0.375 to 0.375
- w_out: bfloat16 [256, 256], replicated, may hold values from -0.375 to 0.375
- mlp_gain: float32 [256], replicated, may hold values from 0.25 to 4
- w_up: bfloat16 [256, 1024], replicated, may hold values from -0.375 to 0.375
- bias_up: float32 [1024], replicated, may hold values from -3 to 3
- w_down: bfloat16 [1024, 256], replicated, may hold values from -0.1875 to 0.1875
Outputs:
- refined: bfloat16 [4, 64, 64, 256], P('date', 'strip', 'groups'), parts along dimension 2
The draws below stay inside these ranges and needn't reach their ends.
There are 2 independent parts, one for each index of `groups`. The reference program is written for one: setup_inputs(seed, part) draws one part's arguments, and reference() takes and returns one part's arrays. A program takes and returns all parts, laid end to end along the dimension named above; an argument that names none is the same for every part. Nothing has to cross between parts.
Inputs may be any that keep to these rules, and one draw needn't show every extreme that they name: `valid_dates`: every pixel has at least one date with value 1.
All inputs are finite; a program needn't handle non-finite values.
Results may differ from the reference program's by a relative error of at most 0.012.
The reference program's roundings to bfloat16 on the way count: a program that leaves them out, or rounds other values in their place, can miss the bound.
Values may be sent and summed in bfloat16 or wider, within the bound.
A program may use at most 64 MiB of HBM per device.

```python
import math
import jax
import jax.numpy as jnp
from jax import lax

C = 256
FFN = 1024
HEADS = 8
HALF = 8
W = 32
DATES = 4
ROWS = 64


def query_key_pair(key):
    base_weight = jax.random.normal(jax.random.fold_in(key, 11), (C, C), jnp.float32) / math.sqrt(C)
    noise_weight = jax.random.normal(jax.random.fold_in(key, 12), (C, C), jnp.float32) / math.sqrt(C)
    query_weight = noise_weight
    return (jnp.clip(query_weight, -20.0, 20.0), jnp.clip(base_weight, -20.0, 20.0))


def draw_w_query(key, part):
    return query_key_pair(key)[0].astype(jnp.bfloat16)


def draw_w_key(key, part):
    return query_key_pair(key)[1].astype(jnp.bfloat16)


def draw_valid_dates(key, part):
    coin = jax.random.randint(jax.random.fold_in(key, 21), (DATES, ROWS, W), 0, 10)
    kept_date = jax.random.randint(jax.random.fold_in(key, 22), (1, ROWS, W), 0, DATES)
    dates_iota = lax.broadcasted_iota(jnp.int32, (DATES, ROWS, W), 0)
    return ((coin < 6) | (dates_iota == kept_date)).astype(jnp.int32)


def levels(rng, dims, pieces, least, largest):
    factor_of, own = 1.0, jax.random.fold_in(rng, 6)
    for dim, blocks in pieces:
        heights = jnp.exp(jax.random.uniform(jax.random.fold_in(own, dim), (blocks,), jnp.float32, least / len(pieces), largest / len(pieces)))
        factor_of = factor_of * jnp.repeat(heights, dims[dim] // blocks).reshape([-1 if axis == dim else 1 for axis in range(len(dims))])
    return factor_of


def normal_values(key, dims, deviation, reach, pieces=(), dtype=jnp.bfloat16):
    level = levels(key, dims, pieces, -0.22, 0.18) if pieces else 1.0
    entries = jax.random.normal(key, dims, jnp.float32) * deviation * level
    return jnp.minimum(jnp.maximum(entries, -reach), reach).astype(dtype)


def setup_inputs(seed: int = 0, part: int = 0) -> dict:
    arg_keys = jax.random.split(jax.random.key(seed), 15)
    part_keys = jax.random.split(jax.random.fold_in(arg_keys[14], part), 15)
    return {
        "features": normal_values(part_keys[0], (DATES, ROWS, W, C), 1.0, 6.0, ((0, 4), (1, 4))),
        "valid_dates": draw_valid_dates(jax.random.fold_in(jax.random.fold_in(arg_keys[14], part), 71), part),
        "conv_weight": normal_values(arg_keys[2], (3, 3, C, C), (3 * C) ** -0.5, 0.21875),
        "conv_bias": normal_values(arg_keys[3], (C,), 0.5, 3.0, (), jnp.float32),
        "fade_table": jnp.clip(jnp.exp(jax.random.uniform(arg_keys[4], (2 * HALF,), jnp.float32, math.log(0.2), math.log(5.0))), 0.2, 5.0),
        "norm_gain": jnp.clip(jnp.exp(jax.random.uniform(arg_keys[5], (C,), jnp.float32, math.log(0.25), math.log(4.0))), 0.25, 4.0),
        "w_query": draw_w_query(jax.random.fold_in(arg_keys[14], 71), part),
        "w_key": draw_w_key(jax.random.fold_in(arg_keys[14], 71), part),
        "w_value": normal_values(arg_keys[8], (C, C), C ** -0.5, 0.375),
        "w_out": normal_values(arg_keys[9], (C, C), C ** -0.5, 0.375),
        "mlp_gain": jnp.clip(jnp.exp(jax.random.uniform(arg_keys[10], (C,), jnp.float32, math.log(0.25), math.log(4.0))), 0.25, 4.0),
        "w_up": normal_values(arg_keys[11], (C, FFN), C ** -0.5, 0.375),
        "bias_up": normal_values(arg_keys[12], (FFN,), 0.5, 3.0, (), jnp.float32),
        "w_down": normal_values(arg_keys[13], (FFN, C), FFN ** -0.5, 0.1875),
    }


eps_norm = 1e-05

def layer_norm(values, norm_scale):
    center = values - lax.optimization_barrier(jnp.mean(values, axis=-1, keepdims=True))
    spread = lax.optimization_barrier(jnp.mean(center * center, axis=-1, keepdims=True))
    return center * lax.rsqrt(spread + eps_norm) * norm_scale

def tile_conv(tile_stack, conv_weight, conv_bias):
    widths = [(0, 0)] * (tile_stack.ndim - 3) + [(1, 1), (1, 1), (0, 0)]
    padded = jnp.pad(tile_stack, widths)
    tile_rows = tile_stack.shape[-3]
    col_count = tile_stack.shape[-2]
    running = None
    for row_shift in range(3):
        for col_shift in range(3):
            window = padded[..., row_shift:row_shift + tile_rows, col_shift:col_shift + col_count, :]
            conv_term = jnp.dot(window, conv_weight[row_shift, col_shift], preferred_element_type=jnp.float32)
            running = conv_term if running is None else running + conv_term
    return running + conv_bias

def blend_halves(lower_half, upper_half, fade_table):
    half_rows = fade_table.shape[0] // 2
    lower_weight = fade_table[half_rows:][:, None, None]
    upper_weight = fade_table[:half_rows][:, None, None]
    return (lower_weight * lower_half + upper_weight * upper_half) / (lower_weight + upper_weight)

def merge_date(date_image, conv_weight, conv_bias, fade_table):
    half_rows = fade_table.shape[0] // 2
    row_count, col_count, chan_count = date_image.shape
    rectified = jnp.maximum(date_image, jnp.zeros((), jnp.bfloat16))
    padded = jnp.pad(rectified, ((half_rows, half_rows), (0, 0), (0, 0)))
    blocks = padded.reshape(-1, half_rows, col_count, chan_count)
    tile_stack = jnp.concatenate([blocks[:-1], blocks[1:]], axis=1)
    tile_outputs = tile_conv(tile_stack, conv_weight, conv_bias)
    blended = blend_halves(tile_outputs[:-1, half_rows:], tile_outputs[1:, :half_rows], fade_table)
    blended = blended.reshape(row_count, col_count, chan_count)
    return (date_image.astype(jnp.float32) + blended).astype(jnp.bfloat16)

def attend(tokens, valid, norm_gain, w_query, w_key, w_value):
    date_count, pixel_count, chan_count = tokens.shape
    head_dim = chan_count // HEADS
    normed = layer_norm(tokens.astype(jnp.float32), norm_gain).astype(jnp.bfloat16)
    shape_heads = (date_count, pixel_count, HEADS, head_dim)
    query_heads = jnp.dot(normed, w_query, preferred_element_type=jnp.float32).astype(jnp.bfloat16).reshape(shape_heads)
    key_heads = jnp.dot(normed, w_key, preferred_element_type=jnp.float32).astype(jnp.bfloat16).reshape(shape_heads)
    value_heads = jnp.dot(normed, w_value, preferred_element_type=jnp.float32).astype(jnp.bfloat16).reshape(shape_heads)
    scores = jnp.einsum('tphd,sphd->phts', query_heads.astype(jnp.float32), key_heads.astype(jnp.float32))
    scores = scores * (1.0 / math.sqrt(head_dim))
    allowed = (jnp.transpose(valid) > 0)[:, None, None, :]
    scores = jnp.where(allowed, scores, -jnp.inf)
    row_max = lax.optimization_barrier(jnp.max(scores, axis=-1, keepdims=True))
    weights = jnp.exp(scores - row_max)
    weights = (weights / lax.optimization_barrier(jnp.sum(weights, axis=-1, keepdims=True))).astype(jnp.bfloat16)
    mixed_heads = jnp.einsum('phts,sphd->tphd', weights.astype(jnp.float32), value_heads.astype(jnp.float32))
    return mixed_heads.astype(jnp.bfloat16).reshape(date_count, pixel_count, chan_count)

def finish(tokens, attended, w_out, mlp_gain, w_up, bias_up, w_down):
    residual = (tokens.astype(jnp.float32) + jnp.dot(attended, w_out, preferred_element_type=jnp.float32)).astype(jnp.bfloat16)
    mlp_in = layer_norm(residual.astype(jnp.float32), mlp_gain).astype(jnp.bfloat16)
    hidden = jax.nn.gelu(jnp.dot(mlp_in, w_up, preferred_element_type=jnp.float32) + bias_up, approximate=True).astype(jnp.bfloat16)
    return (residual.astype(jnp.float32) + jnp.dot(hidden, w_down, preferred_element_type=jnp.float32)).astype(jnp.bfloat16)

def reference(features, valid_dates, conv_weight, conv_bias, fade_table, norm_gain, w_query, w_key, w_value, w_out, mlp_gain, w_up, bias_up, w_down):
    date_count, row_count, col_count, chan_count = features.shape
    merged_rows = lax.map(lambda date_image: merge_date(date_image, conv_weight, conv_bias, fade_table), features)
    tokens = merged_rows.reshape(date_count, row_count * col_count, chan_count)
    valid = valid_dates.reshape(date_count, row_count * col_count)
    attended = attend(tokens, valid, norm_gain, w_query, w_key, w_value)
    refined = finish(tokens, attended, w_out, mlp_gain, w_up, bias_up, w_down)
    return refined.reshape(date_count, row_count, col_count, chan_count)
```

```python
import functools
import math

import jax
import jax.numpy as jnp
from jax import lax
from jax.experimental import pallas as pl
from jax.experimental.pallas import tpu as pltpu
from jax.sharding import PartitionSpec as P

HEADS = 8
GROUPS = (1, 1, 2)
EPS = 1e-05
F32 = jnp.float32
BF16 = jnp.bfloat16
MESH = pl.DeviceIdType.MESH


def norm_rows(values, gain):
    center = values - jnp.mean(values, axis=-1, keepdims=True)
    spread = jnp.mean(center * center, axis=-1, keepdims=True)
    return center * lax.rsqrt(spread + EPS) * gain


def kernel(
    dims,
    feat,
    valid,
    conv_w,
    conv_b_h,
    fade_h,
    gain1_h,
    w_q,
    w_k,
    w_v,
    w_o,
    gain2_h,
    w_up,
    b_up_h,
    w_down,
    out,
    feat_v,
    halo,
    x3,
    stage,
    tok,
    own_mask,
    masks,
    maskcol,
    rowcol,
    qkv,
    att,
    ostage,
    conv_wv,
    w_qkv,
    w_ov,
    w_upv,
    w_downv,
    conv_b,
    fade,
    gain1,
    gain2,
    b_up,
    load_sem,
    halo_send,
    halo_recv,
    mask_send,
    mask_recv,
    send1,
    recv1,
    send2,
    recv2,
):
    dates, strips, rows, cols, chans, half, pieces, unit = dims
    me = lax.axis_index("date")
    strip = lax.axis_index("strip")
    has_up, has_down = strip > 0, strip < strips - 1
    low = me < dates // 2
    order = list(range(1, pieces - 1)) + [0] + ([pieces - 1] if pieces > 1 else [])

    mate = strip + 1 - 2 * lax.rem(strip, 2)
    beyond = 2 * strip - mate
    has_beyond = (beyond >= 0) & (beyond < strips)

    def far(k):
        up = jnp.where(k < me, k, k + 1)
        down = jnp.where(dates - 1 - k > me, dates - 1 - k, dates - 2 - k)
        return jnp.where(k == dates - 1, me, jnp.where(low, down, up))

    loads = [
        pltpu.make_async_copy(src, dst, load_sem.at[i])
        for i, (src, dst) in enumerate(
            [
                (feat, feat_v),
                (conv_b_h, conv_b),
                (fade_h, fade),
                (valid, own_mask),
                (conv_w, conv_wv),
                (w_q, w_qkv.at[:, 0:chans]),
                (w_k, w_qkv.at[:, chans : 2 * chans]),
                (w_v, w_qkv.at[:, 2 * chans : 3 * chans]),
                (w_o, w_ov),
                (w_up, w_upv),
                (w_down, w_downv),
                (gain1_h, gain1),
                (gain2_h, gain2),
                (b_up_h, b_up),
            ]
        )
    ]
    for load in (loads[0], loads[4], loads[1], loads[2], loads[3]):
        load.start()

    barrier = pltpu.get_barrier_semaphore()

    @pl.loop(0, dates)
    def _(k):
        pl.semaphore_signal(
            barrier, inc=1, device_id={"date": far(k), "strip": mate}, device_id_type=MESH
        )

    @pl.when(has_beyond)
    def _():
        pl.semaphore_signal(barrier, inc=1, device_id={"strip": beyond}, device_id_type=MESH)

    chunk_rows = math.gcd(rows, 4)
    chunk_px = chunk_rows * cols

    def spread_columns(block, place):
        count = block.shape[0]
        col = lax.rem(lax.broadcasted_iota(jnp.int32, block.shape, 0), cols)
        block = jnp.maximum(block, 0.0)
        up = jnp.where(col == 0, 0.0, pltpu.roll(block, 1, 0))
        down = jnp.where(col == cols - 1, 0.0, pltpu.roll(block, count - 1, 0))
        x3[pl.ds(place, count), 0:chans] = up.astype(BF16)
        x3[pl.ds(place, count), chans : 2 * chans] = block.astype(BF16)
        x3[pl.ds(place, count), 2 * chans : 3 * chans] = down.astype(BF16)

    x3[0:cols, :] = jnp.zeros((cols, 3 * chans), BF16)
    x3[(rows + 1) * cols : (rows + 2) * cols, :] = jnp.zeros((cols, 3 * chans), BF16)
    loads[0].wait()

    @pl.loop(0, rows // chunk_rows)
    def _(c):
        block = feat_v[pl.ds(pl.multiple_of(c * chunk_px, cols), chunk_px), :]
        spread_columns(block.astype(F32), pl.multiple_of(c * chunk_px + cols, cols))

    def merge_rows(first, count):
        base = first * cols
        if not isinstance(first, int):
            base = pl.multiple_of(base, cols)

        def taps(a):
            return jnp.dot(
                x3[pl.ds(base + a * cols, count * cols), :],
                conv_wv[a],
                preferred_element_type=F32,
            )

        row = lax.broadcasted_iota(jnp.int32, (count * cols, chans), 0) // cols
        row = lax.rem(row + first, half)
        total = taps(1)
        total = total + taps(0) * jnp.where(row == 0, share_up, 1.0)
        total = total + taps(2) * jnp.where(row == half - 1, share_down, 1.0)
        total = total + conv_b[...]
        place = pl.ds(base, count * cols)
        stage[place, :] = (feat_v[place, :].astype(F32) + total).astype(BF16)

    loads[4].wait()
    for load in loads[5:]:
        load.start()
    for load in loads[1:3]:
        load.wait()

    def fade_row(i):
        return jnp.broadcast_to(fade[:, i : i + 1], (1, chans))

    share_up = fade_row(half) / (fade_row(half) + fade_row(0))
    share_down = fade_row(half - 1) / (fade_row(2 * half - 1) + fade_row(half - 1))

    def edge_copy(row, side, peer):
        return pltpu.make_async_remote_copy(
            feat.at[row * cols : (row + 1) * cols, :],
            halo.at[side],
            halo_send.at[side],
            halo_recv.at[side],
            {"strip": peer},
            MESH,
        )

    def mask_copy(peer, slot):
        return pltpu.make_async_remote_copy(
            own_mask,
            masks.at[slot],
            mask_send.at[peer],
            mask_recv.at[slot],
            {"date": peer, "strip": mate},
            MESH,
        )

    def slab(ref, piece, owner):
        return ref.at[pl.ds(pl.multiple_of((piece * dates + owner) * unit, unit), unit), :]

    def piece_at(i):
        if isinstance(i, int):
            return order[i]
        piece = order[0]
        for j, q in enumerate(order[1:], 1):
            piece = jnp.where(i == j, q, piece)
        return piece

    def send_block(i, owner, slot):
        return pltpu.make_async_remote_copy(
            slab(stage, piece_at(i), owner),
            tok.at[i, slot],
            send1.at[i, owner],
            recv1.at[i, slot],
            {"date": owner, "strip": mate},
            MESH,
        )

    def finish_edge(side):
        @pl.when(has_down if side else has_up)
        def _():
            edge_copy(0, side, strip).wait_recv()
            spread_columns(halo[side].astype(F32), (rows + 1) * cols if side else 0)
            merge_rows(rows - 1 if side else 0, 1)

    early = pieces > 1 and unit >= cols
    last = dates - 1

    def start_if(ready, i, owner):
        @pl.when(ready)
        def _():
            send_block(i, owner, me).start()

    piece_rows = rows // pieces

    def merge_piece(piece):
        @pl.loop(0, piece_rows // piece_chunk)
        def _(c):
            merge_rows(piece * piece_rows + c * piece_chunk, piece_chunk)

    piece_chunk = math.gcd(piece_rows, 4)

    def send_piece(i):
        edge_owner = {0: 0, pieces - 1: last}.get(order[i], -1)
        if early or edge_owner < 0:

            @pl.loop(0, dates)
            def _(k):
                start_if(far(k) != edge_owner, i, far(k))

    merge_piece(order[0])
    pl.semaphore_wait(barrier, dates + has_beyond.astype(jnp.int32))

    @pl.when(has_up)
    def _():
        edge_copy(0, 1, strip - 1).start()

    @pl.when(has_down)
    def _():
        edge_copy(rows - 1, 0, strip + 1).start()

    for i in range(pieces):
        if i > 0:
            merge_piece(order[i])
        send_piece(i)
        if i == 0:
            loads[3].wait()

            @pl.loop(0, dates)
            def _(k):
                mask_copy(far(k), me).start()

    for i, piece in enumerate(order):
        if piece == 0:
            finish_edge(0)
        if piece == pieces - 1:
            finish_edge(1)
        if early and piece in (0, pieces - 1):
            edge_owner = 0 if piece == 0 else last
            send_block(i, edge_owner, me).start()
        elif piece in (0, pieces - 1):

            @pl.loop(0, dates)
            def _(k):
                send_block(i, far(k), me).start()

    for load in loads[5:]:
        load.wait()

    width = chans // HEADS
    same_head = (
        lax.rem(lax.broadcasted_iota(jnp.int32, (2 * chans, chans), 0), chans) // width
        == lax.broadcasted_iota(jnp.int32, (2 * chans, chans), 1) // width
    )
    gather = jnp.where(same_head, 1.0, 0.0).astype(BF16)
    eye = lax.broadcasted_iota(jnp.int32, (cols, cols), 0) == lax.broadcasted_iota(
        jnp.int32, (cols, cols), 1
    )
    mask_rows = rowcol.shape[0] // cols
    tokens = dates * unit

    @pl.loop(0, dates)
    def _(k):
        mask_copy(k, k).wait_recv()

    @pl.loop(0, dates)
    def _(s):
        for i, piece in enumerate(order):
            at = (piece * dates + me) * unit
            first_row = at // cols
            for r in range(mask_rows):
                line = masks[s, pl.ds(first_row + r, 1), :].astype(F32)
                column = jnp.sum(jnp.where(eye, line, 0.0), axis=1, keepdims=True)
                rowcol[r * cols : (r + 1) * cols, :] = jnp.broadcast_to(column, (cols, chans))
            offset = pl.multiple_of(at - first_row * cols, math.gcd(unit, cols))
            maskcol[i, s] = rowcol[pl.ds(offset, unit), :]

    group = max(1, min(dates, 512 // tokens))

    def back(i, slot, date):
        return pltpu.make_async_remote_copy(
            ostage.at[i, date],
            slab(out, piece_at(i), slot),
            send2.at[i, date],
            recv2.at[i, slot],
            {"date": date, "strip": mate},
            MESH,
        )

    def attend(i, g, allowed):
        query = qkv[i, pl.ds(g * group, group), :, 0:chans].astype(F32)
        keys = qkv[i, :, :, chans : 2 * chans].astype(F32)
        product = (query[:, None] * keys[None]).reshape(group * tokens, chans)
        head = product.astype(BF16)
        tail = (product - head.astype(F32)).astype(BF16)
        scores = jnp.dot(
            jnp.concatenate([head, tail], axis=1), gather, preferred_element_type=F32
        ) * (1.0 / math.sqrt(width))
        scores = jnp.where(allowed[None], scores.reshape(group, dates, unit, chans), -jnp.inf)
        weights = jnp.exp(scores - jnp.max(scores, axis=1, keepdims=True))
        probs = weights * (1.0 / jnp.sum(weights, axis=1, keepdims=True))
        probs = probs.astype(BF16).astype(F32)
        values = qkv[i, :, :, 2 * chans :].astype(F32)
        att[i, pl.ds(g * group, group)] = jnp.sum(probs * values[None], axis=1).astype(BF16)

    def compute_pieces(first, count):
        span = slice(first, first + count)

        @pl.loop(0, dates)
        def _(k):
            for i in range(first, first + count):
                send_block(i, k, k).wait_recv()

        block = tok[span].reshape(count * tokens, chans)
        normed = norm_rows(block.astype(F32), gain1[...]).astype(BF16)
        qkv[span] = (
            jnp.dot(normed, w_qkv[...], preferred_element_type=F32)
            .astype(BF16)
            .reshape(count, dates, unit, 3 * chans)
        )
        for i in range(first, first + count):
            allowed = maskcol[i] > 0.0
            if group == dates:
                attend(i, 0, allowed)
            else:

                @pl.loop(0, dates // group)
                def _(g):
                    attend(i, g, allowed)

        attended = att[span].reshape(count * tokens, chans)
        residual = (
            block.astype(F32) + jnp.dot(attended, w_ov[...], preferred_element_type=F32)
        ).astype(BF16)
        mlp_in = norm_rows(residual.astype(F32), gain2[...]).astype(BF16)
        hidden = jax.nn.gelu(
            jnp.dot(mlp_in, w_upv[...], preferred_element_type=F32) + b_up[...], approximate=True
        ).astype(BF16)
        ostage[span] = (
            (residual.astype(F32) + jnp.dot(hidden, w_downv[...], preferred_element_type=F32))
            .astype(BF16)
            .reshape(count, dates, unit, chans)
        )

        @pl.loop(0, dates)
        def _(k):
            for i in range(first, first + count):
                back(i, me, far(k)).start()

    done = 0
    for count in GROUPS if sum(GROUPS) == pieces else (1,) * pieces:
        compute_pieces(done, count)
        done += count

    @pl.loop(0, dates)
    def _(k):
        mask_copy(k, me).wait_send()

        @pl.loop(0, pieces)
        def _(piece):
            send_block(piece, k, me).wait_send()
            back(piece, me, k).wait_send()
            back(piece, k, k).wait_recv()

    @pl.when(has_up)
    def _():
        edge_copy(0, 1, strip - 1).wait_send()

    @pl.when(has_down)
    def _():
        edge_copy(rows - 1, 0, strip + 1).wait_send()


def shards(
    features,
    valid_dates,
    conv_weight,
    conv_bias,
    fade_table,
    norm_gain,
    w_query,
    w_key,
    w_value,
    w_out,
    mlp_gain,
    w_up,
    bias_up,
    w_down,
):
    _, rows, cols, chans = features.shape
    hidden = w_up.shape[1]
    half = fade_table.shape[0] // 2
    dates, strips = lax.axis_size("date"), lax.axis_size("strip")
    pixels = rows * cols // dates
    pieces = next(p for p in (4, 2, 1) if p == 1 or (pixels >= 32 * p and rows % p == 0))
    unit = pixels // pieces
    mask_rows = max(1, unit // cols)
    dims = (dates, strips, rows, cols, chans, half, pieces, unit)
    any_spec = pl.BlockSpec(memory_space=pl.ANY)
    vmem = pl.BlockSpec(memory_space=pltpu.VMEM)
    dma = pltpu.SemaphoreType.DMA
    refined = pl.pallas_call(
        functools.partial(kernel, dims),
        out_shape=pltpu.VMEM((rows * cols, chans), BF16),
        in_specs=[any_spec] * 14,
        out_specs=vmem,
        scratch_shapes=[
            pltpu.VMEM((rows * cols, chans), BF16),
            pltpu.VMEM((2, cols, chans), BF16),
            pltpu.VMEM(((rows + 2) * cols, 3 * chans), BF16),
            pltpu.VMEM((rows * cols, chans), BF16),
            pltpu.VMEM((pieces, dates, unit, chans), BF16),
            pltpu.VMEM((rows, cols), jnp.int32),
            pltpu.VMEM((dates, rows, cols), jnp.int32),
            pltpu.VMEM((pieces, dates, unit, chans), F32),
            pltpu.VMEM((mask_rows * cols, chans), F32),
            pltpu.VMEM((pieces, dates, unit, 3 * chans), BF16),
            pltpu.VMEM((pieces, dates, unit, chans), BF16),
            pltpu.VMEM((pieces, dates, unit, chans), BF16),
            pltpu.VMEM((3, 3 * chans, chans), BF16),
            pltpu.VMEM((chans, 3 * chans), BF16),
            pltpu.VMEM((chans, chans), BF16),
            pltpu.VMEM((chans, hidden), BF16),
            pltpu.VMEM((hidden, chans), BF16),
            pltpu.VMEM((1, chans), F32),
            pltpu.VMEM((1, 2 * half), F32),
            pltpu.VMEM((1, chans), F32),
            pltpu.VMEM((1, chans), F32),
            pltpu.VMEM((1, hidden), F32),
            dma((14,)),
            dma((2,)),
            dma((2,)),
            dma((dates,)),
            dma((dates,)),
            dma((pieces, dates)),
            dma((pieces, dates)),
            dma((pieces, dates)),
            dma((pieces, dates)),
        ],
        compiler_params=pltpu.CompilerParams(collective_id=0, has_side_effects=True),
        name="merge_attend",
    )(
        features.reshape(rows * cols, chans),
        valid_dates.reshape(rows, cols),
        conv_weight.reshape(3, 3 * chans, chans),
        conv_bias.reshape(1, chans),
        fade_table.reshape(1, 2 * half),
        norm_gain.reshape(1, chans),
        w_query,
        w_key,
        w_value,
        w_out,
        mlp_gain.reshape(1, chans),
        w_up,
        bias_up.reshape(1, hidden),
        w_down,
    )
    return refined.reshape(1, rows, cols, chans)


def solution(mesh):
    in_specs = (
        P("date", "strip", "groups", None),
        P("date", "strip", "groups"),
    ) + (P(),) * 12
    out_specs = P("date", "strip", "groups", None)
    return jax.shard_map(shards, mesh=mesh, in_specs=in_specs, out_specs=out_specs, check_vma=False)
```

```python
import functools
import math

import jax
import jax.numpy as jnp
from jax import lax
from jax.experimental import pallas as pl
from jax.experimental.pallas import tpu as pltpu
from jax.sharding import PartitionSpec as P

HEADS = 8
GROUPS = (1, 1, 2)
EPS = 1e-05
F32 = jnp.float32
BF16 = jnp.bfloat16
MESH = pl.DeviceIdType.MESH


def norm_rows(values, gain):
    center = values - jnp.mean(values, axis=-1, keepdims=True)
    spread = jnp.mean(center * center, axis=-1, keepdims=True)
    return center * lax.rsqrt(spread + EPS) * gain


def kernel(
    dims,
    feat,
    valid,
    conv_w,
    conv_b_h,
    fade_h,
    gain1_h,
    w_q,
    w_k,
    w_v,
    w_o,
    gain2_h,
    w_up,
    b_up_h,
    w_down,
    out,
    feat_v,
    halo,
    x3,
    stage,
    tok,
    own_mask,
    flag_rows,
    flags,
    maskcol,
    qkv,
    att,
    ostage,
    conv_wv,
    w_qkv,
    w_ov,
    w_upv,
    w_downv,
    conv_b,
    fade,
    gain1,
    gain2,
    b_up,
    load_sem,
    halo_send,
    halo_recv,
    mask_send,
    mask_recv,
    send1,
    recv1,
    send2,
    recv2,
):
    dates, strips, rows, cols, chans, half, pieces, unit = dims
    me = lax.axis_index("date")
    strip = lax.axis_index("strip")
    has_up, has_down = strip > 0, strip < strips - 1
    low = me < dates // 2
    order = list(range(1, pieces - 1)) + [0] + ([pieces - 1] if pieces > 1 else [])

    mate = strip + 1 - 2 * lax.rem(strip, 2)
    beyond = 2 * strip - mate
    has_beyond = (beyond >= 0) & (beyond < strips)

    def far(k):
        up = jnp.where(k < me, k, k + 1)
        down = jnp.where(dates - 1 - k > me, dates - 1 - k, dates - 2 - k)
        return jnp.where(k == dates - 1, me, jnp.where(low, down, up))

    loads = [
        pltpu.make_async_copy(src, dst, load_sem.at[i])
        for i, (src, dst) in enumerate(
            [
                (feat, feat_v),
                (conv_b_h, conv_b),
                (fade_h, fade),
                (valid, own_mask),
                (conv_w, conv_wv),
                (w_q, w_qkv.at[:, 0:chans]),
                (w_k, w_qkv.at[:, chans : 2 * chans]),
                (w_v, w_qkv.at[:, 2 * chans : 3 * chans]),
                (w_o, w_ov),
                (w_up, w_upv),
                (w_down, w_downv),
                (gain1_h, gain1),
                (gain2_h, gain2),
                (b_up_h, b_up),
            ]
        )
    ]
    for load in (loads[0], loads[4], loads[1], loads[2], loads[3]):
        load.start()

    barrier = pltpu.get_barrier_semaphore()

    @pl.loop(0, dates)
    def _(k):
        pl.semaphore_signal(
            barrier, inc=1, device_id={"date": far(k), "strip": mate}, device_id_type=MESH
        )

    @pl.when(has_beyond)
    def _():
        pl.semaphore_signal(barrier, inc=1, device_id={"strip": beyond}, device_id_type=MESH)

    chunk_rows = math.gcd(rows, 4)
    chunk_px = chunk_rows * cols

    def spread_columns(block, place):
        count = block.shape[0]
        col = lax.rem(lax.broadcasted_iota(jnp.int32, block.shape, 0), cols)
        block = jnp.maximum(block, 0.0)
        up = jnp.where(col == 0, 0.0, pltpu.roll(block, 1, 0))
        down = jnp.where(col == cols - 1, 0.0, pltpu.roll(block, count - 1, 0))
        x3[pl.ds(place, count), 0:chans] = up.astype(BF16)
        x3[pl.ds(place, count), chans : 2 * chans] = block.astype(BF16)
        x3[pl.ds(place, count), 2 * chans : 3 * chans] = down.astype(BF16)

    x3[0:cols, :] = jnp.zeros((cols, 3 * chans), BF16)
    x3[(rows + 1) * cols : (rows + 2) * cols, :] = jnp.zeros((cols, 3 * chans), BF16)
    loads[0].wait()

    @pl.loop(0, rows // chunk_rows)
    def _(c):
        block = feat_v[pl.ds(pl.multiple_of(c * chunk_px, cols), chunk_px), :]
        spread_columns(block.astype(F32), pl.multiple_of(c * chunk_px + cols, cols))

    def merge_rows(first, count):
        base = first * cols
        if not isinstance(first, int):
            base = pl.multiple_of(base, cols)

        def taps(a):
            return jnp.dot(
                x3[pl.ds(base + a * cols, count * cols), :],
                conv_wv[a],
                preferred_element_type=F32,
            )

        row = lax.broadcasted_iota(jnp.int32, (count * cols, chans), 0) // cols
        row = lax.rem(row + first, half)
        total = taps(1)
        total = total + taps(0) * jnp.where(row == 0, share_up, 1.0)
        total = total + taps(2) * jnp.where(row == half - 1, share_down, 1.0)
        total = total + conv_b[...]
        place = pl.ds(base, count * cols)
        stage[place, :] = (feat_v[place, :].astype(F32) + total).astype(BF16)

    loads[4].wait()
    for load in loads[5:]:
        load.start()
    for load in loads[1:3]:
        load.wait()

    def fade_row(i):
        return jnp.broadcast_to(fade[:, i : i + 1], (1, chans))

    share_up = fade_row(half) / (fade_row(half) + fade_row(0))
    share_down = fade_row(half - 1) / (fade_row(2 * half - 1) + fade_row(half - 1))

    def edge_copy(row, side, peer):
        return pltpu.make_async_remote_copy(
            feat.at[row * cols : (row + 1) * cols, :],
            halo.at[side],
            halo_send.at[side],
            halo_recv.at[side],
            {"strip": peer},
            MESH,
        )

    def mask_copy(peer, slot):
        return pltpu.make_async_remote_copy(
            flag_rows.at[peer],
            flags.at[slot],
            mask_send.at[peer],
            mask_recv.at[slot],
            {"date": peer, "strip": mate},
            MESH,
        )

    def slab(ref, piece, owner):
        return ref.at[pl.ds(pl.multiple_of((piece * dates + owner) * unit, unit), unit), :]

    def piece_at(i):
        if isinstance(i, int):
            return order[i]
        piece = order[0]
        for j, q in enumerate(order[1:], 1):
            piece = jnp.where(i == j, q, piece)
        return piece

    def send_block(i, owner, slot):
        return pltpu.make_async_remote_copy(
            slab(stage, piece_at(i), owner),
            tok.at[i, slot],
            send1.at[i, owner],
            recv1.at[i, slot],
            {"date": owner, "strip": mate},
            MESH,
        )

    def finish_edge(side):
        @pl.when(has_down if side else has_up)
        def _():
            edge_copy(0, side, strip).wait_recv()
            spread_columns(halo[side].astype(F32), (rows + 1) * cols if side else 0)
            merge_rows(rows - 1 if side else 0, 1)

    early = pieces > 1 and unit >= cols
    last = dates - 1

    def start_if(ready, i, owner):
        @pl.when(ready)
        def _():
            send_block(i, owner, me).start()

    piece_rows = rows // pieces

    def merge_piece(piece):
        @pl.loop(0, piece_rows // piece_chunk)
        def _(c):
            merge_rows(piece * piece_rows + c * piece_chunk, piece_chunk)

    piece_chunk = math.gcd(piece_rows, 4)

    def send_piece(i):
        edge_owner = {0: 0, pieces - 1: last}.get(order[i], -1)
        if early or edge_owner < 0:

            @pl.loop(0, dates)
            def _(k):
                start_if(far(k) != edge_owner, i, far(k))

    def gather_flags():
        step = min(unit, cols)
        pad = flag_rows.shape[2] - pieces * unit
        for owner in range(dates):
            line = []
            for i in range(pieces):
                for at in range((order[i] * dates + owner) * unit, (order[i] * dates + owner + 1) * unit, step):
                    line.append(own_mask[at // cols : at // cols + 1, at % cols : at % cols + step])
            if pad:
                line.append(jnp.zeros((1, pad), jnp.int32))
            flag_rows[owner] = jnp.concatenate(line, axis=1).astype(F32)

    merge_piece(order[0])
    pl.semaphore_wait(barrier, dates + has_beyond.astype(jnp.int32))

    @pl.when(has_up)
    def _():
        edge_copy(0, 1, strip - 1).start()

    @pl.when(has_down)
    def _():
        edge_copy(rows - 1, 0, strip + 1).start()

    for i in range(pieces):
        if i > 0:
            merge_piece(order[i])
        send_piece(i)
        if i == 0:
            loads[3].wait()
            gather_flags()

            @pl.loop(0, dates)
            def _(k):
                mask_copy(far(k), me).start()

    for i, piece in enumerate(order):
        if piece == 0:
            finish_edge(0)
        if piece == pieces - 1:
            finish_edge(1)
        if early and piece in (0, pieces - 1):
            edge_owner = 0 if piece == 0 else last
            send_block(i, edge_owner, me).start()
        elif piece in (0, pieces - 1):

            @pl.loop(0, dates)
            def _(k):
                send_block(i, far(k), me).start()

    for load in loads[5:]:
        load.wait()

    width = chans // HEADS
    same_head = (
        lax.rem(lax.broadcasted_iota(jnp.int32, (2 * chans, chans), 0), chans) // width
        == lax.broadcasted_iota(jnp.int32, (2 * chans, chans), 1) // width
    )
    gather = jnp.where(same_head, 1.0, 0.0).astype(BF16)
    owned = pieces * unit
    eye = lax.broadcasted_iota(jnp.int32, (owned, owned), 0) == lax.broadcasted_iota(
        jnp.int32, (owned, owned), 1
    )
    tokens = dates * unit

    @pl.loop(0, dates)
    def _(k):
        mask_copy(k, k).wait_recv()

    @pl.loop(0, dates)
    def _(s):
        line = flags[s][:, 0:owned]
        column = jnp.sum(jnp.where(eye, line, 0.0), axis=1, keepdims=True)
        wide = jnp.broadcast_to(column, (owned, chans))
        for i in range(pieces):
            maskcol[i, s] = wide[i * unit : (i + 1) * unit, :]

    group = max(1, min(dates, 512 // tokens))

    def back(i, slot, date):
        return pltpu.make_async_remote_copy(
            ostage.at[i, date],
            slab(out, piece_at(i), slot),
            send2.at[i, date],
            recv2.at[i, slot],
            {"date": date, "strip": mate},
            MESH,
        )

    def attend(i, g, allowed):
        query = qkv[i, pl.ds(g * group, group), :, 0:chans].astype(F32)
        keys = qkv[i, :, :, chans : 2 * chans].astype(F32)
        product = (query[:, None] * keys[None]).reshape(group * tokens, chans)
        head = product.astype(BF16)
        tail = (product - head.astype(F32)).astype(BF16)
        scores = jnp.dot(
            jnp.concatenate([head, tail], axis=1), gather, preferred_element_type=F32
        ) * (1.0 / math.sqrt(width))
        scores = jnp.where(allowed[None], scores.reshape(group, dates, unit, chans), -jnp.inf)
        weights = jnp.exp(scores - jnp.max(scores, axis=1, keepdims=True))
        probs = weights * (1.0 / jnp.sum(weights, axis=1, keepdims=True))
        probs = probs.astype(BF16).astype(F32)
        values = qkv[i, :, :, 2 * chans :].astype(F32)
        att[i, pl.ds(g * group, group)] = jnp.sum(probs * values[None], axis=1).astype(BF16)

    def compute_pieces(first, count):
        span = slice(first, first + count)

        @pl.loop(0, dates)
        def _(k):
            for i in range(first, first + count):
                send_block(i, k, k).wait_recv()

        block = tok[span].reshape(count * tokens, chans)
        normed = norm_rows(block.astype(F32), gain1[...]).astype(BF16)
        qkv[span] = (
            jnp.dot(normed, w_qkv[...], preferred_element_type=F32)
            .astype(BF16)
            .reshape(count, dates, unit, 3 * chans)
        )
        for i in range(first, first + count):
            allowed = maskcol[i] > 0.0
            if group == dates:
                attend(i, 0, allowed)
            else:

                @pl.loop(0, dates // group)
                def _(g):
                    attend(i, g, allowed)

        attended = att[span].reshape(count * tokens, chans)
        residual = (
            block.astype(F32) + jnp.dot(attended, w_ov[...], preferred_element_type=F32)
        ).astype(BF16)
        mlp_in = norm_rows(residual.astype(F32), gain2[...]).astype(BF16)
        hidden = jax.nn.gelu(
            jnp.dot(mlp_in, w_upv[...], preferred_element_type=F32) + b_up[...], approximate=True
        ).astype(BF16)
        ostage[span] = (
            (residual.astype(F32) + jnp.dot(hidden, w_downv[...], preferred_element_type=F32))
            .astype(BF16)
            .reshape(count, dates, unit, chans)
        )

        @pl.loop(0, dates)
        def _(k):
            for i in range(first, first + count):
                back(i, me, far(k)).start()

    done = 0
    for count in GROUPS if sum(GROUPS) == pieces else (1,) * pieces:
        compute_pieces(done, count)
        done += count

    @pl.loop(0, dates)
    def _(k):
        mask_copy(k, me).wait_send()

        @pl.loop(0, pieces)
        def _(piece):
            send_block(piece, k, me).wait_send()
            back(piece, me, k).wait_send()
            back(piece, k, k).wait_recv()

    @pl.when(has_up)
    def _():
        edge_copy(0, 1, strip - 1).wait_send()

    @pl.when(has_down)
    def _():
        edge_copy(rows - 1, 0, strip + 1).wait_send()


def shards(
    features,
    valid_dates,
    conv_weight,
    conv_bias,
    fade_table,
    norm_gain,
    w_query,
    w_key,
    w_value,
    w_out,
    mlp_gain,
    w_up,
    bias_up,
    w_down,
):
    _, rows, cols, chans = features.shape
    hidden = w_up.shape[1]
    half = fade_table.shape[0] // 2
    dates, strips = lax.axis_size("date"), lax.axis_size("strip")
    pixels = rows * cols // dates
    pieces = next(p for p in (4, 2, 1) if p == 1 or (pixels >= 32 * p and rows % p == 0))
    unit = pixels // pieces
    lanes = -(-pieces * unit // 128) * 128
    dims = (dates, strips, rows, cols, chans, half, pieces, unit)
    any_spec = pl.BlockSpec(memory_space=pl.ANY)
    vmem = pl.BlockSpec(memory_space=pltpu.VMEM)
    dma = pltpu.SemaphoreType.DMA
    refined = pl.pallas_call(
        functools.partial(kernel, dims),
        out_shape=pltpu.VMEM((rows * cols, chans), BF16),
        in_specs=[any_spec] * 14,
        out_specs=vmem,
        scratch_shapes=[
            pltpu.VMEM((rows * cols, chans), BF16),
            pltpu.VMEM((2, cols, chans), BF16),
            pltpu.VMEM(((rows + 2) * cols, 3 * chans), BF16),
            pltpu.VMEM((rows * cols, chans), BF16),
            pltpu.VMEM((pieces, dates, unit, chans), BF16),
            pltpu.VMEM((rows, cols), jnp.int32),
            pltpu.VMEM((dates, 1, lanes), F32),
            pltpu.VMEM((dates, 1, lanes), F32),
            pltpu.VMEM((pieces, dates, unit, chans), F32),
            pltpu.VMEM((pieces, dates, unit, 3 * chans), BF16),
            pltpu.VMEM((pieces, dates, unit, chans), BF16),
            pltpu.VMEM((pieces, dates, unit, chans), BF16),
            pltpu.VMEM((3, 3 * chans, chans), BF16),
            pltpu.VMEM((chans, 3 * chans), BF16),
            pltpu.VMEM((chans, chans), BF16),
            pltpu.VMEM((chans, hidden), BF16),
            pltpu.VMEM((hidden, chans), BF16),
            pltpu.VMEM((1, chans), F32),
            pltpu.VMEM((1, 2 * half), F32),
            pltpu.VMEM((1, chans), F32),
            pltpu.VMEM((1, chans), F32),
            pltpu.VMEM((1, hidden), F32),
            dma((14,)),
            dma((2,)),
            dma((2,)),
            dma((dates,)),
            dma((dates,)),
            dma((pieces, dates)),
            dma((pieces, dates)),
            dma((pieces, dates)),
            dma((pieces, dates)),
        ],
        compiler_params=pltpu.CompilerParams(collective_id=0, has_side_effects=True),
        name="merge_attend",
    )(
        features.reshape(rows * cols, chans),
        valid_dates.reshape(rows, cols),
        conv_weight.reshape(3, 3 * chans, chans),
        conv_bias.reshape(1, chans),
        fade_table.reshape(1, 2 * half),
        norm_gain.reshape(1, chans),
        w_query,
        w_key,
        w_value,
        w_out,
        mlp_gain.reshape(1, chans),
        w_up,
        bias_up.reshape(1, hidden),
        w_down,
    )
    return refined.reshape(1, rows, cols, chans)


def solution(mesh):
    in_specs = (
        P("date", "strip", "groups", None),
        P("date", "strip", "groups"),
    ) + (P(),) * 12
    out_specs = P("date", "strip", "groups", None)
    return jax.shard_map(shards, mesh=mesh, in_specs=in_specs, out_specs=out_specs, check_vma=False)
```

```python
import functools
import math

import jax
import jax.numpy as jnp
from jax import lax
from jax.experimental import pallas as pl
from jax.experimental.pallas import tpu as pltpu
from jax.sharding import PartitionSpec as P

HEADS = 8
GROUPS = (1, 1, 1, 1)
EPS = 1e-05
F32 = jnp.float32
BF16 = jnp.bfloat16
MESH = pl.DeviceIdType.MESH


def norm_rows(values, gain):
    share = 1.0 / values.shape[-1]
    mean = jnp.sum(values, axis=-1, keepdims=True) * share
    square = jnp.sum(values * values, axis=-1, keepdims=True) * share
    spread = jnp.maximum(square - mean * mean, 0.0)
    return (values - mean) * (lax.rsqrt(spread + EPS) * gain)


def gelu(x):
    slope = math.sqrt(2.0 / math.pi)
    half = 0.5 * x
    return half + half * jnp.tanh(x * (slope + (slope * 0.044715) * (x * x)))


def kernel(
    dims,
    feat,
    valid,
    conv_w,
    conv_b_h,
    fade_h,
    gain1_h,
    w_q,
    w_k,
    w_v,
    w_o,
    gain2_h,
    w_up,
    b_up_h,
    w_down,
    out,
    feat_v,
    halo,
    x3,
    stage,
    tok,
    own_mask,
    flag_rows,
    flags,
    maskcol,
    qkv,
    att,
    ostage,
    conv_wv,
    w_qkv,
    w_ov,
    w_upv,
    w_downv,
    conv_b,
    fade,
    gain1,
    gain2,
    b_up,
    load_sem,
    halo_send,
    halo_recv,
    mask_send,
    mask_recv,
    send1,
    recv1,
    send2,
    recv2,
):
    dates, strips, rows, cols, chans, half, pieces, unit = dims
    me = lax.axis_index("date")
    strip = lax.axis_index("strip")
    has_up, has_down = strip > 0, strip < strips - 1
    low = me < dates // 2
    order = list(range(1, pieces - 1)) + [0] + ([pieces - 1] if pieces > 1 else [])

    mate = strip + 1 - 2 * lax.rem(strip, 2)
    beyond = 2 * strip - mate
    has_beyond = (beyond >= 0) & (beyond < strips)

    def far(k):
        up = jnp.where(k < me, k, k + 1)
        down = jnp.where(dates - 1 - k > me, dates - 1 - k, dates - 2 - k)
        return jnp.where(k == dates - 1, me, jnp.where(low, down, up))

    loads = [
        pltpu.make_async_copy(src, dst, load_sem.at[i])
        for i, (src, dst) in enumerate(
            [
                (feat, feat_v),
                (conv_b_h, conv_b),
                (fade_h, fade),
                (valid, own_mask),
                (conv_w, conv_wv),
                (w_q, w_qkv.at[:, 0:chans]),
                (w_k, w_qkv.at[:, chans : 2 * chans]),
                (w_v, w_qkv.at[:, 2 * chans : 3 * chans]),
                (w_o, w_ov),
                (w_up, w_upv),
                (w_down, w_downv),
                (gain1_h, gain1),
                (gain2_h, gain2),
                (b_up_h, b_up),
            ]
        )
    ]
    for load in (loads[0], loads[4], loads[1], loads[2], loads[3]):
        load.start()

    barrier = pltpu.get_barrier_semaphore()

    @pl.loop(0, dates)
    def _(k):
        pl.semaphore_signal(
            barrier, inc=1, device_id={"date": far(k), "strip": mate}, device_id_type=MESH
        )

    @pl.when(has_beyond)
    def _():
        pl.semaphore_signal(barrier, inc=1, device_id={"strip": beyond}, device_id_type=MESH)

    chunk_rows = math.gcd(rows, 4)
    chunk_px = chunk_rows * cols

    def spread_columns(block, place):
        count = block.shape[0]
        col = lax.rem(lax.broadcasted_iota(jnp.int32, block.shape, 0), cols)
        block = jnp.maximum(block, 0.0)
        up = jnp.where(col == 0, 0.0, pltpu.roll(block, 1, 0))
        down = jnp.where(col == cols - 1, 0.0, pltpu.roll(block, count - 1, 0))
        x3[pl.ds(place, count), 0:chans] = up.astype(BF16)
        x3[pl.ds(place, count), chans : 2 * chans] = block.astype(BF16)
        x3[pl.ds(place, count), 2 * chans : 3 * chans] = down.astype(BF16)

    x3[0:cols, :] = jnp.zeros((cols, 3 * chans), BF16)
    x3[(rows + 1) * cols : (rows + 2) * cols, :] = jnp.zeros((cols, 3 * chans), BF16)
    loads[0].wait()

    @pl.loop(0, rows // chunk_rows)
    def _(c):
        block = feat_v[pl.ds(pl.multiple_of(c * chunk_px, cols), chunk_px), :]
        spread_columns(block.astype(F32), pl.multiple_of(c * chunk_px + cols, cols))

    def merge_rows(first, count):
        base = first * cols
        if not isinstance(first, int):
            base = pl.multiple_of(base, cols)

        def taps(a):
            return jnp.dot(
                x3[pl.ds(base + a * cols, count * cols), :],
                conv_wv[a],
                preferred_element_type=F32,
            )

        row = lax.broadcasted_iota(jnp.int32, (count * cols, chans), 0) // cols
        row = lax.rem(row + first, half)
        total = taps(1)
        total = total + taps(0) * jnp.where(row == 0, share_up, 1.0)
        total = total + taps(2) * jnp.where(row == half - 1, share_down, 1.0)
        total = total + conv_b[...]
        place = pl.ds(base, count * cols)
        stage[place, :] = (feat_v[place, :].astype(F32) + total).astype(BF16)

    loads[4].wait()
    for load in loads[5:]:
        load.start()
    for load in loads[1:3]:
        load.wait()

    def fade_row(i):
        return jnp.broadcast_to(fade[:, i : i + 1], (1, chans))

    share_up = fade_row(half) / (fade_row(half) + fade_row(0))
    share_down = fade_row(half - 1) / (fade_row(2 * half - 1) + fade_row(half - 1))

    def edge_copy(row, side, peer):
        return pltpu.make_async_remote_copy(
            feat.at[row * cols : (row + 1) * cols, :],
            halo.at[side],
            halo_send.at[side],
            halo_recv.at[side],
            {"strip": peer},
            MESH,
        )

    def mask_copy(peer, slot):
        return pltpu.make_async_remote_copy(
            flag_rows.at[peer],
            flags.at[slot],
            mask_send.at[peer],
            mask_recv.at[slot],
            {"date": peer, "strip": mate},
            MESH,
        )

    def slab(ref, piece, owner):
        return ref.at[pl.ds(pl.multiple_of((piece * dates + owner) * unit, unit), unit), :]

    def piece_at(i):
        if isinstance(i, int):
            return order[i]
        piece = order[0]
        for j, q in enumerate(order[1:], 1):
            piece = jnp.where(i == j, q, piece)
        return piece

    def send_block(i, owner, slot):
        return pltpu.make_async_remote_copy(
            slab(stage, piece_at(i), owner),
            tok.at[i, slot],
            send1.at[i, owner],
            recv1.at[i, slot],
            {"date": owner, "strip": mate},
            MESH,
        )

    def finish_edge(side):
        @pl.when(has_down if side else has_up)
        def _():
            edge_copy(0, side, strip).wait_recv()
            spread_columns(halo[side].astype(F32), (rows + 1) * cols if side else 0)
            merge_rows(rows - 1 if side else 0, 1)

    early = pieces > 1 and unit >= cols
    last = dates - 1

    def start_if(ready, i, owner):
        @pl.when(ready)
        def _():
            send_block(i, owner, me).start()

    piece_rows = rows // pieces

    def merge_piece(piece):
        @pl.loop(0, piece_rows // piece_chunk)
        def _(c):
            merge_rows(piece * piece_rows + c * piece_chunk, piece_chunk)

    piece_chunk = math.gcd(piece_rows, 4)

    def send_piece(i):
        edge_owner = {0: 0, pieces - 1: last}.get(order[i], -1)
        if early or edge_owner < 0:

            @pl.loop(0, dates)
            def _(k):
                start_if(far(k) != edge_owner, i, far(k))

    def gather_flags():
        step = min(unit, cols)
        pad = flag_rows.shape[2] - pieces * unit
        for owner in range(dates):
            line = []
            for i in range(pieces):
                for at in range((order[i] * dates + owner) * unit, (order[i] * dates + owner + 1) * unit, step):
                    line.append(own_mask[at // cols : at // cols + 1, at % cols : at % cols + step])
            if pad:
                line.append(jnp.zeros((1, pad), jnp.int32))
            flag_rows[owner] = jnp.concatenate(line, axis=1).astype(F32)

    merge_piece(order[0])
    pl.semaphore_wait(barrier, dates + has_beyond.astype(jnp.int32))

    @pl.when(has_up)
    def _():
        edge_copy(0, 1, strip - 1).start()

    @pl.when(has_down)
    def _():
        edge_copy(rows - 1, 0, strip + 1).start()

    for i in range(pieces):
        if i > 0:
            merge_piece(order[i])
        send_piece(i)
        if i == 0:
            loads[3].wait()
            gather_flags()

            @pl.loop(0, dates)
            def _(k):
                mask_copy(far(k), me).start()

    for i, piece in enumerate(order):
        if piece == 0:
            finish_edge(0)
        if piece == pieces - 1:
            finish_edge(1)
        if early and piece in (0, pieces - 1):
            edge_owner = 0 if piece == 0 else last
            send_block(i, edge_owner, me).start()
        elif piece in (0, pieces - 1):

            @pl.loop(0, dates)
            def _(k):
                send_block(i, far(k), me).start()

    for load in loads[5:]:
        load.wait()

    width = chans // HEADS
    same_head = (
        lax.rem(lax.broadcasted_iota(jnp.int32, (2 * chans, chans), 0), chans) // width
        == lax.broadcasted_iota(jnp.int32, (2 * chans, chans), 1) // width
    )
    gather = jnp.where(same_head, 1.0, 0.0).astype(BF16)
    owned = pieces * unit
    eye = lax.broadcasted_iota(jnp.int32, (owned, owned), 0) == lax.broadcasted_iota(
        jnp.int32, (owned, owned), 1
    )
    tokens = dates * unit

    @pl.loop(0, dates)
    def _(k):
        mask_copy(k, k).wait_recv()

    @pl.loop(0, dates)
    def _(s):
        line = flags[s][:, 0:owned]
        column = jnp.sum(jnp.where(eye, line, 0.0), axis=1, keepdims=True)
        wide = jnp.broadcast_to(column, (owned, chans))
        for i in range(pieces):
            maskcol[i, s] = wide[i * unit : (i + 1) * unit, :]

    def back(i, slot, date):
        return pltpu.make_async_remote_copy(
            ostage.at[i, date],
            slab(out, piece_at(i), slot),
            send2.at[i, date],
            recv2.at[i, slot],
            {"date": date, "strip": mate},
            MESH,
        )

    sharpness = math.log2(math.e) / math.sqrt(width)

    def attend(query, keys, values, allowed):
        product = (query[None] * keys).reshape(tokens, chans)
        head = product.astype(BF16)
        tail = (product - head.astype(F32)).astype(BF16)
        scores = jnp.dot(
            jnp.concatenate([head, tail], axis=1), gather, preferred_element_type=F32
        )
        scores = jnp.where(allowed, scores.reshape(dates, unit, chans), -jnp.inf)
        weights = jnp.exp2((scores - jnp.max(scores, axis=0, keepdims=True)) * sharpness)
        probs = weights * (1.0 / jnp.sum(weights, axis=0, keepdims=True))
        probs = probs.astype(BF16).astype(F32)
        return jnp.sum(probs * values, axis=0).astype(BF16)

    def attend_piece(i, rows_of):
        allowed = maskcol[i] > 0.0
        if dates <= 8:
            query, keys, values = (
                rows_of[:, j * chans : (j + 1) * chans].reshape(dates, unit, chans).astype(F32)
                for j in range(3)
            )
            parts = [attend(query[t], keys, values, allowed) for t in range(dates)]
            return jnp.concatenate(parts, axis=0)
        qkv[...] = rows_of.reshape(dates, unit, 3 * chans)

        @pl.loop(0, dates)
        def _(t):
            query = qkv[t][:, 0:chans].astype(F32)
            keys = qkv[:, :, chans : 2 * chans].astype(F32)
            values = qkv[:, :, 2 * chans :].astype(F32)
            att[t] = attend(query, keys, values, allowed)

        return att[...].reshape(tokens, chans)

    def compute_pieces(first, count):
        span = slice(first, first + count)

        @pl.loop(0, dates)
        def _(k):
            for i in range(first, first + count):
                send_block(i, k, k).wait_recv()

        block = tok[span].reshape(count * tokens, chans)
        normed = norm_rows(block.astype(F32), gain1[...]).astype(BF16)
        projected = jnp.dot(normed, w_qkv[...], preferred_element_type=F32).astype(BF16)
        attended = jnp.concatenate(
            [
                attend_piece(first + j, projected[j * tokens : (j + 1) * tokens])
                for j in range(count)
            ],
            axis=0,
        )
        residual = (
            block.astype(F32) + jnp.dot(attended, w_ov[...], preferred_element_type=F32)
        ).astype(BF16)
        mlp_in = norm_rows(residual.astype(F32), gain2[...]).astype(BF16)
        total = residual.astype(F32)
        depth = w_upv.shape[1]
        chunk = depth // 4 if depth % 1024 == 0 else depth
        for j in range(0, depth, chunk):
            part = slice(j, j + chunk)
            hidden = jnp.dot(mlp_in, w_upv[:, part], preferred_element_type=F32) + b_up[:, part]
            total = total + jnp.dot(
                gelu(hidden).astype(BF16), w_downv[part, :], preferred_element_type=F32
            )
        ostage[span] = total.astype(BF16).reshape(count, dates, unit, chans)

        @pl.loop(0, dates)
        def _(k):
            for i in range(first, first + count):
                back(i, me, far(k)).start()

    done = 0
    for count in GROUPS if sum(GROUPS) == pieces else (1,) * pieces:
        compute_pieces(done, count)
        done += count

    @pl.loop(0, dates)
    def _(k):
        mask_copy(k, me).wait_send()

        @pl.loop(0, pieces)
        def _(piece):
            send_block(piece, k, me).wait_send()
            back(piece, me, k).wait_send()
            back(piece, k, k).wait_recv()

    @pl.when(has_up)
    def _():
        edge_copy(0, 1, strip - 1).wait_send()

    @pl.when(has_down)
    def _():
        edge_copy(rows - 1, 0, strip + 1).wait_send()


def shards(
    features,
    valid_dates,
    conv_weight,
    conv_bias,
    fade_table,
    norm_gain,
    w_query,
    w_key,
    w_value,
    w_out,
    mlp_gain,
    w_up,
    bias_up,
    w_down,
):
    _, rows, cols, chans = features.shape
    hidden = w_up.shape[1]
    half = fade_table.shape[0] // 2
    dates, strips = lax.axis_size("date"), lax.axis_size("strip")
    pixels = rows * cols // dates
    pieces = next(p for p in (4, 2, 1) if p == 1 or (pixels >= 32 * p and rows % p == 0))
    unit = pixels // pieces
    lanes = -(-pieces * unit // 128) * 128
    dims = (dates, strips, rows, cols, chans, half, pieces, unit)
    any_spec = pl.BlockSpec(memory_space=pl.ANY)
    vmem = pl.BlockSpec(memory_space=pltpu.VMEM)
    dma = pltpu.SemaphoreType.DMA
    refined = pl.pallas_call(
        functools.partial(kernel, dims),
        out_shape=pltpu.VMEM((rows * cols, chans), BF16),
        in_specs=[any_spec] * 14,
        out_specs=vmem,
        scratch_shapes=[
            pltpu.VMEM((rows * cols, chans), BF16),
            pltpu.VMEM((2, cols, chans), BF16),
            pltpu.VMEM(((rows + 2) * cols, 3 * chans), BF16),
            pltpu.VMEM((rows * cols, chans), BF16),
            pltpu.VMEM((pieces, dates, unit, chans), BF16),
            pltpu.VMEM((rows, cols), jnp.int32),
            pltpu.VMEM((dates, 1, lanes), F32),
            pltpu.VMEM((dates, 1, lanes), F32),
            pltpu.VMEM((pieces, dates, unit, chans), F32),
            pltpu.VMEM((dates, unit, 3 * chans), BF16),
            pltpu.VMEM((dates, unit, chans), BF16),
            pltpu.VMEM((pieces, dates, unit, chans), BF16),
            pltpu.VMEM((3, 3 * chans, chans), BF16),
            pltpu.VMEM((chans, 3 * chans), BF16),
            pltpu.VMEM((chans, chans), BF16),
            pltpu.VMEM((chans, hidden), BF16),
            pltpu.VMEM((hidden, chans), BF16),
            pltpu.VMEM((1, chans), F32),
            pltpu.VMEM((1, 2 * half), F32),
            pltpu.VMEM((1, chans), F32),
            pltpu.VMEM((1, chans), F32),
            pltpu.VMEM((1, hidden), F32),
            dma((14,)),
            dma((2,)),
            dma((2,)),
            dma((dates,)),
            dma((dates,)),
            dma((pieces, dates)),
            dma((pieces, dates)),
            dma((pieces, dates)),
            dma((pieces, dates)),
        ],
        compiler_params=pltpu.CompilerParams(collective_id=0, has_side_effects=True),
        name="merge_attend",
    )(
        features.reshape(rows * cols, chans),
        valid_dates.reshape(rows, cols),
        conv_weight.reshape(3, 3 * chans, chans),
        conv_bias.reshape(1, chans),
        fade_table.reshape(1, 2 * half),
        norm_gain.reshape(1, chans),
        w_query,
        w_key,
        w_value,
        w_out,
        mlp_gain.reshape(1, chans),
        w_up,
        bias_up.reshape(1, hidden),
        w_down,
    )
    return refined.reshape(1, rows, cols, chans)


def solution(mesh):
    in_specs = (
        P("date", "strip", "groups", None),
        P("date", "strip", "groups"),
    ) + (P(),) * 12
    out_specs = P("date", "strip", "groups", None)
    return jax.shard_map(shards, mesh=mesh, in_specs=in_specs, out_specs=out_specs, check_vma=False)
```

```python
import functools
import math

import jax
import jax.numpy as jnp
from jax import lax
from jax.experimental import pallas as pl
from jax.experimental.pallas import tpu as pltpu
from jax.sharding import PartitionSpec as P

HEADS = 8
GROUPS = (1, 1, 1, 1)
EPS = 1e-05
F32 = jnp.float32
BF16 = jnp.bfloat16
MESH = pl.DeviceIdType.MESH


def norm_rows(values, gain):
    share = 1.0 / values.shape[-1]
    mean = jnp.sum(values, axis=-1, keepdims=True) * share
    square = jnp.sum(values * values, axis=-1, keepdims=True) * share
    spread = jnp.maximum(square - mean * mean, 0.0)
    return (values - mean) * (lax.rsqrt(spread + EPS) * gain)


def gelu(x):
    slope = math.sqrt(2.0 / math.pi)
    half = 0.5 * x
    return half + half * jnp.tanh(x * (slope + (slope * 0.044715) * (x * x)))


def kernel(
    dims,
    feat,
    valid,
    conv_w,
    conv_b_h,
    fade_h,
    gain1_h,
    w_q,
    w_k,
    w_v,
    w_o,
    gain2_h,
    w_up,
    b_up_h,
    w_down,
    out,
    feat_v,
    halo,
    x3,
    edge_sum,
    stage,
    tok,
    own_mask,
    flag_rows,
    flags,
    maskcol,
    qkv,
    att,
    ostage,
    conv_wv,
    w_qkv,
    w_ov,
    w_upv,
    w_downv,
    conv_b,
    fade,
    gain1,
    gain2,
    b_up,
    load_sem,
    halo_send,
    halo_recv,
    mask_send,
    mask_recv,
    send1,
    recv1,
    send2,
    recv2,
):
    dates, strips, rows, cols, chans, half, pieces, unit = dims
    me = lax.axis_index("date")
    strip = lax.axis_index("strip")
    has_up, has_down = strip > 0, strip < strips - 1
    low = me < dates // 2
    order = list(range(1, pieces - 1)) + [0] + ([pieces - 1] if pieces > 1 else [])

    mate = strip + 1 - 2 * lax.rem(strip, 2)
    beyond = 2 * strip - mate
    has_beyond = (beyond >= 0) & (beyond < strips)

    def far(k):
        up = jnp.where(k < me, k, k + 1)
        down = jnp.where(dates - 1 - k > me, dates - 1 - k, dates - 2 - k)
        return jnp.where(k == dates - 1, me, jnp.where(low, down, up))

    loads = [
        pltpu.make_async_copy(src, dst, load_sem.at[i])
        for i, (src, dst) in enumerate(
            [
                (feat, feat_v),
                (conv_b_h, conv_b),
                (fade_h, fade),
                (valid, own_mask),
                (conv_w, conv_wv),
                (w_q, w_qkv.at[:, 0:chans]),
                (w_k, w_qkv.at[:, chans : 2 * chans]),
                (w_v, w_qkv.at[:, 2 * chans : 3 * chans]),
                (w_o, w_ov),
                (w_up, w_upv),
                (w_down, w_downv),
                (gain1_h, gain1),
                (gain2_h, gain2),
                (b_up_h, b_up),
            ]
        )
    ]
    for load in (loads[0], loads[4], loads[1], loads[2], loads[3]):
        load.start()

    barrier = pltpu.get_barrier_semaphore()

    @pl.loop(0, dates)
    def _(k):
        pl.semaphore_signal(
            barrier, inc=1, device_id={"date": far(k), "strip": mate}, device_id_type=MESH
        )

    @pl.when(has_beyond)
    def _():
        pl.semaphore_signal(barrier, inc=1, device_id={"strip": beyond}, device_id_type=MESH)

    chunk_rows = math.gcd(rows, 4)
    chunk_px = chunk_rows * cols

    def spread_columns(block, place):
        count = block.shape[0]
        col = lax.rem(lax.broadcasted_iota(jnp.int32, block.shape, 0), cols)
        block = jnp.maximum(block, 0.0)
        up = jnp.where(col == 0, 0.0, pltpu.roll(block, 1, 0))
        down = jnp.where(col == cols - 1, 0.0, pltpu.roll(block, count - 1, 0))
        x3[pl.ds(place, count), 0:chans] = up.astype(BF16)
        x3[pl.ds(place, count), chans : 2 * chans] = block.astype(BF16)
        x3[pl.ds(place, count), 2 * chans : 3 * chans] = down.astype(BF16)

    x3[0:cols, :] = jnp.zeros((cols, 3 * chans), BF16)
    x3[(rows + 1) * cols : (rows + 2) * cols, :] = jnp.zeros((cols, 3 * chans), BF16)
    loads[0].wait()

    @pl.loop(0, rows // chunk_rows)
    def _(c):
        block = feat_v[pl.ds(pl.multiple_of(c * chunk_px, cols), chunk_px), :]
        spread_columns(block.astype(F32), pl.multiple_of(c * chunk_px + cols, cols))

    def merge_rows(first, count):
        base = first * cols
        if not isinstance(first, int):
            base = pl.multiple_of(base, cols)

        def taps(a):
            return jnp.dot(
                x3[pl.ds(base + a * cols, count * cols), :],
                conv_wv[a],
                preferred_element_type=F32,
            )

        row = lax.broadcasted_iota(jnp.int32, (count * cols, chans), 0) // cols
        row = lax.rem(row + first, half)
        total = taps(1)
        total = total + taps(0) * jnp.where(row == 0, share_up, 1.0)
        total = total + taps(2) * jnp.where(row == half - 1, share_down, 1.0)
        total = total + conv_b[...]

        @pl.when(first == 0)
        def _():
            edge_sum[0] = total[0:cols]

        @pl.when(first + count == rows)
        def _():
            edge_sum[1] = total[(count - 1) * cols :]

        place = pl.ds(base, count * cols)
        stage[place, :] = (feat_v[place, :].astype(F32) + total).astype(BF16)

    loads[4].wait()
    for load in loads[5:]:
        load.start()
    for load in loads[1:3]:
        load.wait()

    def fade_row(i):
        return jnp.broadcast_to(fade[:, i : i + 1], (1, chans))

    share_up = fade_row(half) / (fade_row(half) + fade_row(0))
    share_down = fade_row(half - 1) / (fade_row(2 * half - 1) + fade_row(half - 1))

    def edge_copy(row, side, peer):
        return pltpu.make_async_remote_copy(
            feat.at[row * cols : (row + 1) * cols, :],
            halo.at[side],
            halo_send.at[side],
            halo_recv.at[side],
            {"strip": peer},
            MESH,
        )

    def mask_copy(peer, slot):
        return pltpu.make_async_remote_copy(
            flag_rows.at[peer],
            flags.at[slot],
            mask_send.at[peer],
            mask_recv.at[slot],
            {"date": peer, "strip": mate},
            MESH,
        )

    def slab(ref, piece, owner):
        return ref.at[pl.ds(pl.multiple_of((piece * dates + owner) * unit, unit), unit), :]

    def piece_at(i):
        if isinstance(i, int):
            return order[i]
        piece = order[0]
        for j, q in enumerate(order[1:], 1):
            piece = jnp.where(i == j, q, piece)
        return piece

    def send_block(i, owner, slot):
        return pltpu.make_async_remote_copy(
            slab(stage, piece_at(i), owner),
            tok.at[i, slot],
            send1.at[i, owner],
            recv1.at[i, slot],
            {"date": owner, "strip": mate},
            MESH,
        )

    def finish_edge(side):
        @pl.when(has_down if side else has_up)
        def _():
            edge_copy(0, side, strip).wait_recv()
            spread_columns(halo[side].astype(F32), (rows + 1) * cols if side else 0)
            beside = (rows + 1) * cols if side else 0
            row = (rows - 1) * cols if side else 0
            extra = jnp.dot(
                x3[beside : beside + cols, :], conv_wv[2 * side], preferred_element_type=F32
            ) * (share_down if side else share_up)
            total = edge_sum[side] + extra
            stage[row : row + cols, :] = (
                feat_v[row : row + cols, :].astype(F32) + total
            ).astype(BF16)

    early = pieces > 1 and unit >= cols
    last = dates - 1

    def start_if(ready, i, owner):
        @pl.when(ready)
        def _():
            send_block(i, owner, me).start()

    piece_rows = rows // pieces

    def merge_piece(piece):
        @pl.loop(0, piece_rows // piece_chunk)
        def _(c):
            merge_rows(piece * piece_rows + c * piece_chunk, piece_chunk)

    piece_chunk = math.gcd(piece_rows, 4)

    def send_piece(i):
        edge_owner = {0: 0, pieces - 1: last}.get(order[i], -1)
        if early or edge_owner < 0:

            @pl.loop(0, dates)
            def _(k):
                start_if(far(k) != edge_owner, i, far(k))

    def gather_flags():
        step = min(unit, cols)
        pad = flag_rows.shape[2] - pieces * unit
        for owner in range(dates):
            line = []
            for i in range(pieces):
                for at in range((order[i] * dates + owner) * unit, (order[i] * dates + owner + 1) * unit, step):
                    line.append(own_mask[at // cols : at // cols + 1, at % cols : at % cols + step])
            if pad:
                line.append(jnp.zeros((1, pad), jnp.int32))
            flag_rows[owner] = jnp.concatenate(line, axis=1).astype(F32)

    merge_piece(order[0])
    pl.semaphore_wait(barrier, dates + has_beyond.astype(jnp.int32))

    @pl.when(has_up)
    def _():
        edge_copy(0, 1, strip - 1).start()

    @pl.when(has_down)
    def _():
        edge_copy(rows - 1, 0, strip + 1).start()

    for i in range(pieces):
        if i > 0:
            merge_piece(order[i])
        send_piece(i)
        if i == 0:
            loads[3].wait()
            gather_flags()

            @pl.loop(0, dates)
            def _(k):
                mask_copy(far(k), me).start()

    for i, piece in enumerate(order):
        if piece == 0:
            finish_edge(0)
        if piece == pieces - 1:
            finish_edge(1)
        if early and piece in (0, pieces - 1):
            edge_owner = 0 if piece == 0 else last
            send_block(i, edge_owner, me).start()
        elif piece in (0, pieces - 1):

            @pl.loop(0, dates)
            def _(k):
                send_block(i, far(k), me).start()

    for load in loads[5:]:
        load.wait()

    width = chans // HEADS
    same_head = (
        lax.rem(lax.broadcasted_iota(jnp.int32, (2 * chans, chans), 0), chans) // width
        == lax.broadcasted_iota(jnp.int32, (2 * chans, chans), 1) // width
    )
    gather = jnp.where(same_head, 1.0, 0.0).astype(BF16)
    owned = pieces * unit
    eye = lax.broadcasted_iota(jnp.int32, (owned, owned), 0) == lax.broadcasted_iota(
        jnp.int32, (owned, owned), 1
    )
    tokens = dates * unit

    @pl.loop(0, dates)
    def _(k):
        mask_copy(k, k).wait_recv()

    @pl.loop(0, dates)
    def _(s):
        line = flags[s][:, 0:owned]
        column = jnp.sum(jnp.where(eye, line, 0.0), axis=1, keepdims=True)
        wide = jnp.broadcast_to(column, (owned, chans))
        for i in range(pieces):
            maskcol[i, s] = wide[i * unit : (i + 1) * unit, :]

    def back(i, slot, date):
        return pltpu.make_async_remote_copy(
            ostage.at[i, date],
            slab(out, piece_at(i), slot),
            send2.at[i, date],
            recv2.at[i, slot],
            {"date": date, "strip": mate},
            MESH,
        )

    sharpness = math.log2(math.e) / math.sqrt(width)

    def attend(query, keys, values, allowed):
        product = (query[None] * keys).reshape(tokens, chans)
        head = product.astype(BF16)
        tail = (product - head.astype(F32)).astype(BF16)
        scores = jnp.dot(
            jnp.concatenate([head, tail], axis=1), gather, preferred_element_type=F32
        )
        scores = jnp.where(allowed, scores.reshape(dates, unit, chans), -jnp.inf)
        weights = jnp.exp2((scores - jnp.max(scores, axis=0, keepdims=True)) * sharpness)
        probs = weights * (1.0 / jnp.sum(weights, axis=0, keepdims=True))
        probs = probs.astype(BF16).astype(F32)
        return jnp.sum(probs * values, axis=0).astype(BF16)

    def attend_piece(i, rows_of):
        allowed = maskcol[i] > 0.0
        if dates <= 8:
            query, keys, values = (
                rows_of[:, j * chans : (j + 1) * chans].reshape(dates, unit, chans).astype(F32)
                for j in range(3)
            )
            parts = [attend(query[t], keys, values, allowed) for t in range(dates)]
            return jnp.concatenate(parts, axis=0)
        qkv[...] = rows_of.reshape(dates, unit, 3 * chans)

        @pl.loop(0, dates)
        def _(t):
            query = qkv[t][:, 0:chans].astype(F32)
            keys = qkv[:, :, chans : 2 * chans].astype(F32)
            values = qkv[:, :, 2 * chans :].astype(F32)
            att[t] = attend(query, keys, values, allowed)

        return att[...].reshape(tokens, chans)

    def compute_pieces(first, count):
        span = slice(first, first + count)

        @pl.loop(0, dates)
        def _(k):
            for i in range(first, first + count):
                send_block(i, k, k).wait_recv()

        block = tok[span].reshape(count * tokens, chans)
        normed = norm_rows(block.astype(F32), gain1[...]).astype(BF16)
        projected = jnp.dot(normed, w_qkv[...], preferred_element_type=F32).astype(BF16)
        attended = jnp.concatenate(
            [
                attend_piece(first + j, projected[j * tokens : (j + 1) * tokens])
                for j in range(count)
            ],
            axis=0,
        )
        residual = (
            block.astype(F32) + jnp.dot(attended, w_ov[...], preferred_element_type=F32)
        ).astype(BF16)
        mlp_in = norm_rows(residual.astype(F32), gain2[...]).astype(BF16)
        total = residual.astype(F32)
        depth = w_upv.shape[1]
        chunk = depth // 4 if depth % 1024 == 0 else depth
        for j in range(0, depth, chunk):
            part = slice(j, j + chunk)
            hidden = jnp.dot(mlp_in, w_upv[:, part], preferred_element_type=F32) + b_up[:, part]
            total = total + jnp.dot(
                gelu(hidden).astype(BF16), w_downv[part, :], preferred_element_type=F32
            )
        ostage[span] = total.astype(BF16).reshape(count, dates, unit, chans)

        @pl.loop(0, dates)
        def _(k):
            for i in range(first, first + count):
                back(i, me, far(k)).start()

    done = 0
    for count in GROUPS if sum(GROUPS) == pieces else (1,) * pieces:
        compute_pieces(done, count)
        done += count

    @pl.loop(0, dates)
    def _(k):
        mask_copy(k, me).wait_send()

        @pl.loop(0, pieces)
        def _(piece):
            send_block(piece, k, me).wait_send()
            back(piece, me, k).wait_send()
            back(piece, k, k).wait_recv()

    @pl.when(has_up)
    def _():
        edge_copy(0, 1, strip - 1).wait_send()

    @pl.when(has_down)
    def _():
        edge_copy(rows - 1, 0, strip + 1).wait_send()


def shards(
    features,
    valid_dates,
    conv_weight,
    conv_bias,
    fade_table,
    norm_gain,
    w_query,
    w_key,
    w_value,
    w_out,
    mlp_gain,
    w_up,
    bias_up,
    w_down,
):
    _, rows, cols, chans = features.shape
    hidden = w_up.shape[1]
    half = fade_table.shape[0] // 2
    dates, strips = lax.axis_size("date"), lax.axis_size("strip")
    pixels = rows * cols // dates
    pieces = next(p for p in (4, 2, 1) if p == 1 or (pixels >= 32 * p and rows % p == 0))
    unit = pixels // pieces
    lanes = -(-pieces * unit // 128) * 128
    dims = (dates, strips, rows, cols, chans, half, pieces, unit)
    any_spec = pl.BlockSpec(memory_space=pl.ANY)
    vmem = pl.BlockSpec(memory_space=pltpu.VMEM)
    dma = pltpu.SemaphoreType.DMA
    refined = pl.pallas_call(
        functools.partial(kernel, dims),
        out_shape=pltpu.VMEM((rows * cols, chans), BF16),
        in_specs=[any_spec] * 14,
        out_specs=vmem,
        scratch_shapes=[
            pltpu.VMEM((rows * cols, chans), BF16),
            pltpu.VMEM((2, cols, chans), BF16),
            pltpu.VMEM(((rows + 2) * cols, 3 * chans), BF16),
            pltpu.VMEM((2, cols, chans), F32),
            pltpu.VMEM((rows * cols, chans), BF16),
            pltpu.VMEM((pieces, dates, unit, chans), BF16),
            pltpu.VMEM((rows, cols), jnp.int32),
            pltpu.VMEM((dates, 1, lanes), F32),
            pltpu.VMEM((dates, 1, lanes), F32),
            pltpu.VMEM((pieces, dates, unit, chans), F32),
            pltpu.VMEM((dates, unit, 3 * chans), BF16),
            pltpu.VMEM((dates, unit, chans), BF16),
            pltpu.VMEM((pieces, dates, unit, chans), BF16),
            pltpu.VMEM((3, 3 * chans, chans), BF16),
            pltpu.VMEM((chans, 3 * chans), BF16),
            pltpu.VMEM((chans, chans), BF16),
            pltpu.VMEM((chans, hidden), BF16),
            pltpu.VMEM((hidden, chans), BF16),
            pltpu.VMEM((1, chans), F32),
            pltpu.VMEM((1, 2 * half), F32),
            pltpu.VMEM((1, chans), F32),
            pltpu.VMEM((1, chans), F32),
            pltpu.VMEM((1, hidden), F32),
            dma((14,)),
            dma((2,)),
            dma((2,)),
            dma((dates,)),
            dma((dates,)),
            dma((pieces, dates)),
            dma((pieces, dates)),
            dma((pieces, dates)),
            dma((pieces, dates)),
        ],
        compiler_params=pltpu.CompilerParams(collective_id=0, has_side_effects=True),
        name="merge_attend",
    )(
        features.reshape(rows * cols, chans),
        valid_dates.reshape(rows, cols),
        conv_weight.reshape(3, 3 * chans, chans),
        conv_bias.reshape(1, chans),
        fade_table.reshape(1, 2 * half),
        norm_gain.reshape(1, chans),
        w_query,
        w_key,
        w_value,
        w_out,
        mlp_gain.reshape(1, chans),
        w_up,
        bias_up.reshape(1, hidden),
        w_down,
    )
    return refined.reshape(1, rows, cols, chans)


def solution(mesh):
    in_specs = (
        P("date", "strip", "groups", None),
        P("date", "strip", "groups"),
    ) + (P(),) * 12
    out_specs = P("date", "strip", "groups", None)
    return jax.shard_map(shards, mesh=mesh, in_specs=in_specs, out_specs=out_specs, check_vma=False)
```

```python
import functools
import math

import jax
import jax.numpy as jnp
from jax import lax
from jax.experimental import pallas as pl
from jax.experimental.pallas import tpu as pltpu
from jax.sharding import PartitionSpec as P

HEADS = 8
GROUPS = (1, 1, 1, 1)
EPS = 1e-05
F32 = jnp.float32
BF16 = jnp.bfloat16
MESH = pl.DeviceIdType.MESH


def norm_rows(values, gain):
    share = 1.0 / values.shape[-1]
    mean = jnp.sum(values, axis=-1, keepdims=True) * share
    square = jnp.sum(values * values, axis=-1, keepdims=True) * share
    spread = jnp.maximum(square - mean * mean, 0.0)
    return (values - mean) * (lax.rsqrt(spread + EPS) * gain)


def gelu(x):
    slope = math.sqrt(2.0 / math.pi)
    half = 0.5 * x
    return half + half * jnp.tanh(x * (slope + (slope * 0.044715) * (x * x)))


def kernel(
    dims,
    feat,
    valid,
    conv_w,
    conv_b_h,
    fade_h,
    gain1_h,
    w_q,
    w_k,
    w_v,
    w_o,
    gain2_h,
    w_up,
    b_up_h,
    w_down,
    out,
    feat_v,
    halo,
    x3,
    edge_sum,
    stage,
    tok,
    own_mask,
    flag_rows,
    flags,
    maskcol,
    qkv,
    att,
    ostage,
    conv_wv,
    w_qkv,
    w_ov,
    w_upv,
    w_downv,
    conv_b,
    fade,
    gain1,
    gain2,
    b_up,
    load_sem,
    halo_send,
    halo_recv,
    mask_send,
    mask_recv,
    send1,
    recv1,
    send2,
    recv2,
):
    dates, strips, rows, cols, chans, half, pieces, unit = dims
    me = lax.axis_index("date")
    strip = lax.axis_index("strip")
    has_up, has_down = strip > 0, strip < strips - 1
    low = me < dates // 2
    order = list(range(1, pieces - 1)) + [0] + ([pieces - 1] if pieces > 1 else [])

    mate = strip + 1 - 2 * lax.rem(strip, 2)
    beyond = 2 * strip - mate
    has_beyond = (beyond >= 0) & (beyond < strips)

    def far(k):
        up = jnp.where(k < me, k, k + 1)
        down = jnp.where(dates - 1 - k > me, dates - 1 - k, dates - 2 - k)
        return jnp.where(k == dates - 1, me, jnp.where(low, down, up))

    loads = [
        pltpu.make_async_copy(src, dst, load_sem.at[i])
        for i, (src, dst) in enumerate(
            [
                (feat, feat_v),
                (conv_b_h, conv_b),
                (fade_h, fade),
                (valid, own_mask),
                (conv_w, conv_wv),
                (w_q, w_qkv.at[:, 0:chans]),
                (w_k, w_qkv.at[:, chans : 2 * chans]),
                (w_v, w_qkv.at[:, 2 * chans : 3 * chans]),
                (w_o, w_ov),
                (w_up, w_upv),
                (w_down, w_downv),
                (gain1_h, gain1),
                (gain2_h, gain2),
                (b_up_h, b_up),
            ]
        )
    ]
    for load in (loads[0], loads[4], loads[3], loads[1], loads[2]):
        load.start()

    barrier = pltpu.get_barrier_semaphore()

    @pl.loop(0, dates)
    def _(k):
        pl.semaphore_signal(
            barrier, inc=1, device_id={"date": far(k), "strip": mate}, device_id_type=MESH
        )

    @pl.when(has_beyond)
    def _():
        pl.semaphore_signal(barrier, inc=1, device_id={"strip": beyond}, device_id_type=MESH)

    chunk_rows = math.gcd(rows, 4)
    chunk_px = chunk_rows * cols

    def gather_flags():
        step = min(unit, cols)
        pad = flag_rows.shape[2] - pieces * unit
        for owner in range(dates):
            line = []
            for i in range(pieces):
                for at in range((order[i] * dates + owner) * unit, (order[i] * dates + owner + 1) * unit, step):
                    line.append(own_mask[at // cols : at // cols + 1, at % cols : at % cols + step])
            if pad:
                line.append(jnp.zeros((1, pad), jnp.int32))
            flag_rows[owner] = jnp.concatenate(line, axis=1).astype(F32)

    def spread_columns(block, place):
        count = block.shape[0]
        col = lax.rem(lax.broadcasted_iota(jnp.int32, block.shape, 0), cols)
        block = jnp.maximum(block, 0.0)
        up = jnp.where(col == 0, 0.0, pltpu.roll(block, 1, 0))
        down = jnp.where(col == cols - 1, 0.0, pltpu.roll(block, count - 1, 0))
        x3[pl.ds(place, count), 0:chans] = up.astype(BF16)
        x3[pl.ds(place, count), chans : 2 * chans] = block.astype(BF16)
        x3[pl.ds(place, count), 2 * chans : 3 * chans] = down.astype(BF16)

    loads[3].wait()
    gather_flags()
    x3[0:cols, :] = jnp.zeros((cols, 3 * chans), BF16)
    x3[(rows + 1) * cols : (rows + 2) * cols, :] = jnp.zeros((cols, 3 * chans), BF16)
    loads[0].wait()

    @pl.loop(0, rows // chunk_rows)
    def _(c):
        block = feat_v[pl.ds(pl.multiple_of(c * chunk_px, cols), chunk_px), :]
        spread_columns(block.astype(F32), pl.multiple_of(c * chunk_px + cols, cols))

    def merge_rows(first, count):
        base = first * cols
        if not isinstance(first, int):
            base = pl.multiple_of(base, cols)

        def taps(a):
            return jnp.dot(
                x3[pl.ds(base + a * cols, count * cols), :],
                conv_wv[a],
                preferred_element_type=F32,
            )

        row = lax.broadcasted_iota(jnp.int32, (count * cols, chans), 0) // cols
        row = lax.rem(row + first, half)
        total = taps(1)
        total = total + taps(0) * jnp.where(row == 0, share_up, 1.0)
        total = total + taps(2) * jnp.where(row == half - 1, share_down, 1.0)
        total = total + conv_b[...]

        @pl.when(first == 0)
        def _():
            edge_sum[0] = total[0:cols]

        @pl.when(first + count == rows)
        def _():
            edge_sum[1] = total[(count - 1) * cols :]

        place = pl.ds(base, count * cols)
        stage[place, :] = (feat_v[place, :].astype(F32) + total).astype(BF16)

    loads[4].wait()
    for load in loads[5:]:
        load.start()
    for load in loads[1:3]:
        load.wait()

    def fade_row(i):
        return jnp.broadcast_to(fade[:, i : i + 1], (1, chans))

    share_up = fade_row(half) / (fade_row(half) + fade_row(0))
    share_down = fade_row(half - 1) / (fade_row(2 * half - 1) + fade_row(half - 1))

    def edge_copy(row, side, peer):
        return pltpu.make_async_remote_copy(
            feat.at[row * cols : (row + 1) * cols, :],
            halo.at[side],
            halo_send.at[side],
            halo_recv.at[side],
            {"strip": peer},
            MESH,
        )

    def mask_copy(peer, slot):
        return pltpu.make_async_remote_copy(
            flag_rows.at[peer],
            flags.at[slot],
            mask_send.at[peer],
            mask_recv.at[slot],
            {"date": peer, "strip": mate},
            MESH,
        )

    def slab(ref, piece, owner):
        return ref.at[pl.ds(pl.multiple_of((piece * dates + owner) * unit, unit), unit), :]

    def piece_at(i):
        if isinstance(i, int):
            return order[i]
        piece = order[0]
        for j, q in enumerate(order[1:], 1):
            piece = jnp.where(i == j, q, piece)
        return piece

    def send_block(i, owner, slot):
        return pltpu.make_async_remote_copy(
            slab(stage, piece_at(i), owner),
            tok.at[i, slot],
            send1.at[i, owner],
            recv1.at[i, slot],
            {"date": owner, "strip": mate},
            MESH,
        )

    def finish_edge(side):
        @pl.when(has_down if side else has_up)
        def _():
            edge_copy(0, side, strip).wait_recv()
            spread_columns(halo[side].astype(F32), (rows + 1) * cols if side else 0)
            beside = (rows + 1) * cols if side else 0
            row = (rows - 1) * cols if side else 0
            extra = jnp.dot(
                x3[beside : beside + cols, :], conv_wv[2 * side], preferred_element_type=F32
            ) * (share_down if side else share_up)
            total = edge_sum[side] + extra
            stage[row : row + cols, :] = (
                feat_v[row : row + cols, :].astype(F32) + total
            ).astype(BF16)

    early = pieces > 1 and unit >= cols
    last = dates - 1

    def start_if(ready, i, owner):
        @pl.when(ready)
        def _():
            send_block(i, owner, me).start()

    piece_rows = rows // pieces

    def merge_piece(piece):
        @pl.loop(0, piece_rows // piece_chunk)
        def _(c):
            merge_rows(piece * piece_rows + c * piece_chunk, piece_chunk)

    piece_chunk = math.gcd(piece_rows, 4)

    def send_piece(i):
        edge_owner = {0: 0, pieces - 1: last}.get(order[i], -1)
        if early or edge_owner < 0:

            @pl.loop(0, dates)
            def _(k):
                start_if(far(k) != edge_owner, i, far(k))

    merge_piece(order[0])
    pl.semaphore_wait(barrier, dates + has_beyond.astype(jnp.int32))

    @pl.when(has_up)
    def _():
        edge_copy(0, 1, strip - 1).start()

    @pl.when(has_down)
    def _():
        edge_copy(rows - 1, 0, strip + 1).start()

    for i in range(pieces):
        if i > 0:
            merge_piece(order[i])
        send_piece(i)
        if i == 0:

            @pl.loop(0, dates)
            def _(k):
                mask_copy(far(k), me).start()

    for i, piece in enumerate(order):
        if piece == 0:
            finish_edge(0)
        if piece == pieces - 1:
            finish_edge(1)
        if early and piece in (0, pieces - 1):
            edge_owner = 0 if piece == 0 else last
            send_block(i, edge_owner, me).start()
        elif piece in (0, pieces - 1):

            @pl.loop(0, dates)
            def _(k):
                send_block(i, far(k), me).start()

    for load in loads[5:]:
        load.wait()

    width = chans // HEADS
    same_head = (
        lax.rem(lax.broadcasted_iota(jnp.int32, (2 * chans, chans), 0), chans) // width
        == lax.broadcasted_iota(jnp.int32, (2 * chans, chans), 1) // width
    )
    gather = jnp.where(same_head, 1.0, 0.0).astype(BF16)
    owned = pieces * unit
    eye = lax.broadcasted_iota(jnp.int32, (owned, owned), 0) == lax.broadcasted_iota(
        jnp.int32, (owned, owned), 1
    )
    tokens = dates * unit

    @pl.loop(0, dates)
    def _(k):
        mask_copy(k, k).wait_recv()

    @pl.loop(0, dates)
    def _(s):
        line = flags[s][:, 0:owned]
        column = jnp.sum(jnp.where(eye, line, 0.0), axis=1, keepdims=True)
        wide = jnp.broadcast_to(column, (owned, chans))
        for i in range(pieces):
            maskcol[i, s] = wide[i * unit : (i + 1) * unit, :]

    def back(i, slot, date):
        return pltpu.make_async_remote_copy(
            ostage.at[i, date],
            slab(out, piece_at(i), slot),
            send2.at[i, date],
            recv2.at[i, slot],
            {"date": date, "strip": mate},
            MESH,
        )

    sharpness = math.log2(math.e) / math.sqrt(width)

    def attend(query, keys, values, allowed):
        product = (query[None] * keys).reshape(tokens, chans)
        head = product.astype(BF16)
        tail = (product - head.astype(F32)).astype(BF16)
        scores = jnp.dot(
            jnp.concatenate([head, tail], axis=1), gather, preferred_element_type=F32
        )
        scores = jnp.where(allowed, scores.reshape(dates, unit, chans), -jnp.inf)
        weights = jnp.exp2((scores - jnp.max(scores, axis=0, keepdims=True)) * sharpness)
        probs = weights * (1.0 / jnp.sum(weights, axis=0, keepdims=True))
        probs = probs.astype(BF16).astype(F32)
        return jnp.sum(probs * values, axis=0).astype(BF16)

    def attend_piece(i, rows_of):
        allowed = maskcol[i] > 0.0
        if dates <= 8:
            query, keys, values = (
                rows_of[:, j * chans : (j + 1) * chans].reshape(dates, unit, chans).astype(F32)
                for j in range(3)
            )
            parts = [attend(query[t], keys, values, allowed) for t in range(dates)]
            return jnp.concatenate(parts, axis=0)
        qkv[...] = rows_of.reshape(dates, unit, 3 * chans)

        @pl.loop(0, dates)
        def _(t):
            query = qkv[t][:, 0:chans].astype(F32)
            keys = qkv[:, :, chans : 2 * chans].astype(F32)
            values = qkv[:, :, 2 * chans :].astype(F32)
            att[t] = attend(query, keys, values, allowed)

        return att[...].reshape(tokens, chans)

    def compute_pieces(first, count):
        span = slice(first, first + count)

        @pl.loop(0, dates)
        def _(k):
            for i in range(first, first + count):
                send_block(i, k, k).wait_recv()

        block = tok[span].reshape(count * tokens, chans)
        normed = norm_rows(block.astype(F32), gain1[...]).astype(BF16)
        projected = jnp.dot(normed, w_qkv[...], preferred_element_type=F32).astype(BF16)
        attended = jnp.concatenate(
            [
                attend_piece(first + j, projected[j * tokens : (j + 1) * tokens])
                for j in range(count)
            ],
            axis=0,
        )
        residual = (
            block.astype(F32) + jnp.dot(attended, w_ov[...], preferred_element_type=F32)
        ).astype(BF16)
        mlp_in = norm_rows(residual.astype(F32), gain2[...]).astype(BF16)
        total = residual.astype(F32)
        depth = w_upv.shape[1]
        chunk = depth // 4 if depth % 1024 == 0 else depth
        for j in range(0, depth, chunk):
            part = slice(j, j + chunk)
            hidden = jnp.dot(mlp_in, w_upv[:, part], preferred_element_type=F32) + b_up[:, part]
            total = total + jnp.dot(
                gelu(hidden).astype(BF16), w_downv[part, :], preferred_element_type=F32
            )
        ostage[span] = total.astype(BF16).reshape(count, dates, unit, chans)

        @pl.loop(0, dates)
        def _(k):
            for i in range(first, first + count):
                back(i, me, far(k)).start()

    done = 0
    for count in GROUPS if sum(GROUPS) == pieces else (1,) * pieces:
        compute_pieces(done, count)
        done += count

    @pl.loop(0, dates)
    def _(k):
        mask_copy(k, me).wait_send()

        @pl.loop(0, pieces)
        def _(piece):
            send_block(piece, k, me).wait_send()
            back(piece, me, k).wait_send()
            back(piece, k, k).wait_recv()

    @pl.when(has_up)
    def _():
        edge_copy(0, 1, strip - 1).wait_send()

    @pl.when(has_down)
    def _():
        edge_copy(rows - 1, 0, strip + 1).wait_send()


def shards(
    features,
    valid_dates,
    conv_weight,
    conv_bias,
    fade_table,
    norm_gain,
    w_query,
    w_key,
    w_value,
    w_out,
    mlp_gain,
    w_up,
    bias_up,
    w_down,
):
    _, rows, cols, chans = features.shape
    hidden = w_up.shape[1]
    half = fade_table.shape[0] // 2
    dates, strips = lax.axis_size("date"), lax.axis_size("strip")
    pixels = rows * cols // dates
    pieces = next(p for p in (4, 2, 1) if p == 1 or (pixels >= 32 * p and rows % p == 0))
    unit = pixels // pieces
    lanes = -(-pieces * unit // 128) * 128
    dims = (dates, strips, rows, cols, chans, half, pieces, unit)
    any_spec = pl.BlockSpec(memory_space=pl.ANY)
    vmem = pl.BlockSpec(memory_space=pltpu.VMEM)
    dma = pltpu.SemaphoreType.DMA
    refined = pl.pallas_call(
        functools.partial(kernel, dims),
        out_shape=pltpu.VMEM((rows * cols, chans), BF16),
        in_specs=[any_spec] * 14,
        out_specs=vmem,
        scratch_shapes=[
            pltpu.VMEM((rows * cols, chans), BF16),
            pltpu.VMEM((2, cols, chans), BF16),
            pltpu.VMEM(((rows + 2) * cols, 3 * chans), BF16),
            pltpu.VMEM((2, cols, chans), F32),
            pltpu.VMEM((rows * cols, chans), BF16),
            pltpu.VMEM((pieces, dates, unit, chans), BF16),
            pltpu.VMEM((rows, cols), jnp.int32),
            pltpu.VMEM((dates, 1, lanes), F32),
            pltpu.VMEM((dates, 1, lanes), F32),
            pltpu.VMEM((pieces, dates, unit, chans), F32),
            pltpu.VMEM((dates, unit, 3 * chans), BF16),
            pltpu.VMEM((dates, unit, chans), BF16),
            pltpu.VMEM((pieces, dates, unit, chans), BF16),
            pltpu.VMEM((3, 3 * chans, chans), BF16),
            pltpu.VMEM((chans, 3 * chans), BF16),
            pltpu.VMEM((chans, chans), BF16),
            pltpu.VMEM((chans, hidden), BF16),
            pltpu.VMEM((hidden, chans), BF16),
            pltpu.VMEM((1, chans), F32),
            pltpu.VMEM((1, 2 * half), F32),
            pltpu.VMEM((1, chans), F32),
            pltpu.VMEM((1, chans), F32),
            pltpu.VMEM((1, hidden), F32),
            dma((14,)),
            dma((2,)),
            dma((2,)),
            dma((dates,)),
            dma((dates,)),
            dma((pieces, dates)),
            dma((pieces, dates)),
            dma((pieces, dates)),
            dma((pieces, dates)),
        ],
        compiler_params=pltpu.CompilerParams(collective_id=0, has_side_effects=True),
        name="merge_attend",
    )(
        features.reshape(rows * cols, chans),
        valid_dates.reshape(rows, cols),
        conv_weight.reshape(3, 3 * chans, chans),
        conv_bias.reshape(1, chans),
        fade_table.reshape(1, 2 * half),
        norm_gain.reshape(1, chans),
        w_query,
        w_key,
        w_value,
        w_out,
        mlp_gain.reshape(1, chans),
        w_up,
        bias_up.reshape(1, hidden),
        w_down,
    )
    return refined.reshape(1, rows, cols, chans)


def solution(mesh):
    in_specs = (
        P("date", "strip", "groups", None),
        P("date", "strip", "groups"),
    ) + (P(),) * 12
    out_specs = P("date", "strip", "groups", None)
    return jax.shard_map(shards, mesh=mesh, in_specs=in_specs, out_specs=out_specs, check_vma=False)
```
